512 devices in a mesh: batch: 16 (over y, x_lo), centre: 32 (over z, x_hi, core).
Axes of the slice: x: 4 (x_hi: 2, x_lo: 2; x = x_hi * 2 + x_lo), y: 8, z: 8, core: 2. Of those that a mesh axis runs over, the one named last changes fastest.
Arguments:
- batch_pool: bfloat16 [20992, 1024], P(('batch', 'centre')), may hold values from -6 to 6
- batch_index: int32 [16384], P(('batch', 'centre')), may hold values from 0 to 20991, as said below
- centre_pool: bfloat16 [73760, 1024], P('centre'), may hold values from -6 to 6
- centre_index: int32 [65536], P('centre'), may hold values from 0 to 73759, as said below
- targets: float32 [16384, 301], P(('batch', 'centre')), may hold values from -6 to 6
- coefficients: float32 [65536, 301], P('centre'), may hold values from -1.5 to 1.5
Outputs:
- updated: float32 [65536, 301], P('centre')
- residual: float32 [16384, 301], P(('batch', 'centre'))
The draws below stay inside these ranges and needn't reach their ends.
Inputs may be any that keep to these rules, and one draw needn't show every extreme that they name: `batch_index`: the entries of each aligned block of 32 are distinct and lie in the same aligned block of 41 pool rows, block for block. `centre_index`: the entries of each aligned block of 2048 are distinct and lie in the same aligned block of 2305 pool rows, block for block.
All inputs are finite; a program needn't handle non-finite values.
Results may differ from the reference program's by a relative error of at most 0.0034.
Values may be sent and summed in bfloat16 or wider, within the bound.
A program may use at most 64 MiB of HBM per device.

```python
import math
import jax
import jax.numpy as jnp
from jax import lax

D = 1024
OUT = 301
ROWS_DEV = 32
CEN_DEV = 2048
ROW_POOL = 41
CEN_POOL = 2305
BATCH = 16384
CENTRES = 65536
BATCH_POOL = 20992
CENTRE_POOL = 73760
N_BATCH = 16


def feature_rows(base_key, row_constant, numbers):
    cluster_total = min(256, CENTRE_POOL // 8)
    places = 1.0 + jnp.arange(D, dtype=jnp.float32)
    harmonic = jnp.sum(1.0 / places)
    scales = 1.0 / jnp.sqrt(places * harmonic)
    mean_key = jax.random.fold_in(base_key, 21)
    rows_key = jax.random.fold_in(base_key, row_constant)
    means = jnp.clip(jax.random.normal(mean_key, (cluster_total, D), jnp.float32), -3.5, 3.5)
    spread = jnp.ones((cluster_total,), jnp.float32)
    means = 3.4641016 * means

    def one_row(number):
        row_key = jax.random.fold_in(rows_key, number)
        cluster = jax.random.randint(jax.random.fold_in(row_key, 1), (), 0, cluster_total)
        noise_key = jax.random.fold_in(row_key, 2)
        noise = jnp.clip(jax.random.normal(noise_key, (D,), jnp.float32), -4.0, 4.0)
        values = means[cluster] + 0.70710678 * spread[cluster] * noise
        return values * scales
    rows = jax.vmap(one_row)(numbers)
    return jnp.clip(rows, -6.0, 6.0).astype(jnp.bfloat16)


def pick_indices(key, blocks, pool_size, count):

    def one_block(number):
        order = jax.random.permutation(jax.random.fold_in(key, number), pool_size)
        return order[:count].astype(jnp.int32) + number * pool_size
    return jax.vmap(one_block)(jnp.arange(blocks, dtype=jnp.int32)).reshape(-1)


def draw_batch_pool(key, part):
    numbers = jnp.arange(BATCH_POOL, dtype=jnp.int32)
    own_rows = feature_rows(key, 11, numbers)
    sources = jax.random.randint(jax.random.fold_in(key, 15), (BATCH_POOL,), 0, CENTRE_POOL)
    copied = feature_rows(key, 12, sources)
    picked = numbers % 8 == 0
    return jnp.where(picked[:, None], copied, own_rows)


def draw_centre_pool(key, part):
    return feature_rows(key, 12, jnp.arange(CENTRE_POOL, dtype=jnp.int32))


def draw_batch_index(key, part):
    return pick_indices(jax.random.fold_in(key, 13), BATCH_POOL // ROW_POOL, ROW_POOL, ROWS_DEV)


def draw_centre_index(key, part):
    return pick_indices(jax.random.fold_in(key, 14), CENTRE_POOL // CEN_POOL, CEN_POOL, CEN_DEV)


def levels(key, dims, cuts, least, high):
    loudness = 1.0
    for axis_at, shards_of in cuts:
        steps = jax.random.uniform(jax.random.fold_in(jax.random.fold_in(key, 6), axis_at), (shards_of,), jnp.float32, least / len(cuts), high / len(cuts))
        loudness = loudness * jnp.repeat(jnp.exp(steps), dims[axis_at] // shards_of).reshape((-1,) + (1,) * (len(dims) - 1 - axis_at))
    return loudness


def scatter_about(own_key, shape, scale, reach, split=(), kind=jnp.bfloat16):
    array = scale * jax.random.normal(own_key, shape, jnp.float32)
    if split:
        array = array * levels(own_key, shape, split, -0.22, 0.18)
    return jnp.clip(array, -reach, reach).astype(kind)


def setup_inputs(seed: int = 0) -> dict:
    arg_keys = jax.random.split(jax.random.key(seed), 7)
    batch_pool = draw_batch_pool(jax.random.fold_in(arg_keys[6], 71), 0)
    batch_index = draw_batch_index(jax.random.fold_in(arg_keys[6], 71), 0)
    centre_pool = draw_centre_pool(jax.random.fold_in(arg_keys[6], 71), 0)
    centre_index = draw_centre_index(jax.random.fold_in(arg_keys[6], 71), 0)
    targets = scatter_about(arg_keys[4], (BATCH, OUT), 1.0, 6.0, ((0, 512),), jnp.float32)
    coefficients = scatter_about(arg_keys[5], (CENTRES, OUT), 0.25, 1.5, ((0, 32),), jnp.float32)
    return {"batch_pool": batch_pool, "batch_index": batch_index, "centre_pool": centre_pool, "centre_index": centre_index, "targets": targets, "coefficients": coefficients}


def kernel_block(samples, centres, centre_square):
    cross = jnp.dot(samples, centres.T, preferred_element_type=jnp.float32)
    wide = samples.astype(jnp.float32)
    sample_square = lax.optimization_barrier(jnp.sum(wide * wide, axis=1))
    squared = sample_square[:, None] + centre_square[None, :] - 2.0 * cross
    return jnp.exp(-jnp.sqrt(jnp.maximum(squared, 0.0))).astype(jnp.bfloat16)

def reference(batch_pool, batch_index, centre_pool, centre_index, targets, coefficients):
    samples = batch_pool[batch_index]
    centres = centre_pool[centre_index]
    centre_wide = centres.astype(jnp.float32)
    centre_square = lax.optimization_barrier(jnp.sum(centre_wide * centre_wide, axis=1))
    coefficient_half = coefficients.astype(jnp.bfloat16)
    blocks = N_BATCH
    span = samples.shape[0] // blocks
    sample_blocks = samples.reshape(blocks, span, samples.shape[1])
    target_blocks = targets.reshape(blocks, span, targets.shape[1])

    def advance(total, pair):
        block_rows, block_targets = pair
        kernel = kernel_block(block_rows, centres, centre_square)
        prediction = jnp.dot(kernel, coefficient_half, preferred_element_type=jnp.float32)
        residual = prediction - block_targets
        total = total + jnp.dot(kernel.T, residual.astype(jnp.bfloat16), preferred_element_type=jnp.float32)
        return (total, residual)
    start_total = jnp.zeros((centres.shape[0], coefficients.shape[1]), jnp.float32)
    gradient, residual = lax.scan(advance, start_total, (sample_blocks, target_blocks))
    updated = coefficients - 8.0 / math.sqrt(BATCH) * gradient
    return (updated, residual.reshape(BATCH, coefficients.shape[1]))
```

```python
import functools
import math

import jax
import jax.numpy as jnp
from jax import lax
from jax.experimental import pallas as pl
from jax.experimental.pallas import tpu as pltpu
from jax.sharding import PartitionSpec as P

MESH = pl.DeviceIdType.MESH
F32 = jnp.float32
BF16 = jnp.bfloat16
RING = 8
NT = (((1,), (1,)), ((), ()))
NN = (((1,), (0,)), ((), ()))
TN = (((0,), (0,)), ((), ()))
PLACE = (0, 2, 4, 6, 1, 7, 5, 3)
COPIES = 128


def up(n, k):
    return -(-n // k) * k


def dot(a, b, dims):
    return lax.dot_general(a, b, dims, preferred_element_type=F32)


def step_kernel(
    zs, ys, bidx, bpool, cidx, cpool, tgt, coef, grad_out, res_out,
    bsel, xall, pool, tailp, cs, oht, coefv, coefb, coefp, kt, predv, psend, precv,
    qsend, qrecv, tg, tt, res, rq, rt, gp, gpb, ysend, yrecv, fin, xsend, xrecv, grad,
    ssem, rsem, lsem, osem,
):
    bi = lax.axis_index("batch")
    ci = lax.axis_index("centre")
    y, xl = bi // 2, bi % 2
    z, x, c = ci // 4, (ci // 2) % 2, ci % 2
    rows, d = tgt.shape[0], bpool.shape[1]
    out = tgt.shape[1]
    cen = cidx.shape[1]
    n_pool = cpool.shape[0]
    pp = kt.shape[0]
    pm = n_pool // 256 * 256
    lanes = 4 * rows
    half, quart = predv.shape[0] // 2, predv.shape[0] // 4
    og = gp.shape[0]
    cut = up(og // 2, 16)
    chunk = cen // RING
    sub = chunk // 2

    def at(z_, x_, c_):
        return (bi, lax.rem(z_ + 2 * RING, RING) * 4 + x_ * 2 + c_)

    def at_y(y_, xl_):
        return (lax.rem(y_ + 2 * RING, RING) * 2 + xl_, ci)

    count = [0]
    started = []

    def send(src, dst, dev):
        n = count[0]
        count[0] += 1
        copy = pltpu.make_async_remote_copy(
            src_ref=src, dst_ref=dst, send_sem=ssem.at[n], recv_sem=rsem.at[n],
            device_id=dev, device_id_type=MESH,
        )
        copy.start()
        started.append(copy)
        return copy

    partner = at(z, x, 1 - c)
    facing = at(z, 1 - x, c)
    across = at(z, 1 - x, 1 - c)
    greet = []
    if zs:
        greet += [partner, facing, across]
        greet += [at(z + s, x, c) for s in range(1, RING)]
        greet += [at(z + s, 1 - x, c) for s in range(1, RING)]
    if ys:
        greet += [at_y(y + 1, xl), at_y(y - 1, xl), at_y(y, 1 - xl)]
    barrier = pltpu.get_barrier_semaphore()
    for dev in greet:
        pl.semaphore_signal(barrier, inc=1, device_id=dev, device_id_type=MESH)

    load_pool = pltpu.make_async_copy(cpool, pool, lsem.at[0])
    load_pool.start()
    load_coef = pltpu.make_async_copy(coef, coefv, lsem.at[1])
    load_coef.start()

    def rows_at(k):
        return pl.ds(pl.multiple_of(k * rows, rows), rows)

    def quart_at(k):
        return pl.ds(pl.multiple_of(k * quart, 16), quart)

    def half_at(k):
        return pl.ds(pl.multiple_of(k * half, 16), half)

    j = c * 2 + x
    jx = c * 2 + 1 - x

    bsel[...] = jnp.zeros_like(bsel)
    bsel[0 : bpool.shape[0], :] = bpool[...]
    base = (bi * lax.axis_size("centre") + ci) * bpool.shape[0]
    place = lax.broadcasted_iota(jnp.int32, (bsel.shape[0], rows), 0) + base
    pick = jnp.where(place == bidx[...], -2.0, 0.0).astype(BF16)
    xall[0, rows_at(j), :] = dot(pick, bsel[...], TN).astype(BF16)
    tg[rows_at(j), :] = jnp.zeros((rows, tg.shape[1]), F32)
    tg[rows_at(j), 0:out] = tgt[...]

    pl.semaphore_wait(barrier, len(greet))

    ring = {}
    mate = {}
    if zs:
        own = xall.at[0, rows_at(j)]
        cross_x = send(own, own, facing)
        for way, slot in ((1, RING - 1), (-1, 1)):
            ring[way, 1, 0] = send(own, xall.at[PLACE[slot], rows_at(j)], at(z + way, x, c))
        mate[0, 0] = send(own, own, partner)
        mine = tg.at[rows_at(j)]
        tg_sent = [send(mine, mine, dev) for dev in (partner, facing, across)]

    def slot_of(way, level):
        return RING - level if way == 1 else level

    def forward(level):
        if not zs:
            return
        for stream, place_of in ((0, j), (1, jx)):
            for way in (1, -1):
                if level == 0:
                    if way == 1:
                        if stream == 0:
                            continue
                        cross_x.wait_recv()
                        block = xall.at[0, rows_at(jx)]
                        mate[0, 1] = send(block, block, partner)
                    elif stream == 0:
                        continue
                else:
                    if level == 4 and (way == 1) != (stream == 0):
                        continue
                    ring[way, level, stream].wait_recv()
                slot = slot_of(way, level) % RING
                block = xall.at[PLACE[slot], rows_at(place_of)]
                if level < 4 and (level < 3 or (way == 1) == (stream == 0)):
                    nxt = slot_of(way, level + 1)
                    ring[way, level + 1, stream] = send(
                        block, xall.at[PLACE[nxt], rows_at(place_of)], at(z + way, x, c)
                    )
                if level:
                    mate[slot, stream] = send(block, block, partner)

    def ready(slots):
        if zs:
            for s in slots:
                mate[s, 0].wait_recv()
                mate[s, 1].wait_recv()

    cbase = ci * n_pool
    step_rows = 32

    def build(m, carry):
        r0 = pl.multiple_of(m * step_rows, step_rows)
        at_row = lax.broadcasted_iota(jnp.int32, (step_rows, cen), 0) + (cbase + r0)
        oht[pl.ds(r0, step_rows), :] = jnp.where(at_row == cidx[...], 1.0, 0.0).astype(BF16)
        return carry

    lax.fori_loop(0, pp // step_rows, build, 0)
    forward(0)

    load_coef.wait()
    coefb[...] = jnp.zeros_like(coefb)
    coefb[0:out, :] = coefv[...].astype(BF16)
    if og < coefp.shape[0]:
        coefp[og:, :] = jnp.zeros_like(coefp[og:, :])

    def permute(n, width):
        n = pl.multiple_of(n, 128)
        coefp[0:og, pl.ds(n, width)] = dot(
            coefb[...], oht[pl.ds(n, width), :], NT
        ).astype(BF16)

    def permute_body(m, carry):
        permute(m * 256, 256)
        return carry

    lax.fori_loop(0, pm // 256, permute_body, 0)
    permute(pm, pp - pm)
    forward(1)

    load_pool.wait()
    tailp[...] = jnp.zeros_like(tailp)
    tailp[0 : n_pool - pm, :] = pool[pm:n_pool, :]

    def squares(m, carry):
        r0 = pl.multiple_of(m * 128, 128)
        wide = pool[pl.ds(r0, 128), :].astype(F32)
        cs[pl.ds(r0, 128), :] = jnp.broadcast_to(
            jnp.sum(wide * wide, axis=1, keepdims=True), (128, 128)
        )
        return carry

    lax.fori_loop(0, pm // 128, squares, 0)
    wide_tail = tailp[...].astype(F32)
    cs_tail = jnp.sum(wide_tail * wide_tail, axis=1, keepdims=True)
    kt[pm:, :] = jnp.zeros_like(kt[pm:, :])

    def near(squared):
        return jnp.exp(-jnp.sqrt(jnp.maximum(squared, 0.0))).astype(BF16)

    def kernel_of(p0, n):
        width = n * lanes
        cols = slice(p0 * lanes, p0 * lanes + width)
        feats = xall[p0 : p0 + n].reshape(width, d)
        wide = feats.astype(F32)
        square = wide * wide * 0.25
        high = square.astype(BF16)
        low = (square - high.astype(F32)).astype(BF16)
        ones = jnp.ones((16, d), BF16)
        row = (dot(ones, high, NT) + dot(ones, low, NT))[0:1, :]

        def body(m, carry):
            r0 = pl.multiple_of(m * 256, 256)
            both = dot(pool[pl.ds(r0, 256), :], xall[p0 : p0 + n].reshape(width, d), NT)
            col = cs[pl.ds(r0, 256), :]
            col = jnp.concatenate([col] * (width // 128), axis=1) if width > 128 else col[:, :width]
            kt[pl.ds(r0, 256), cols] = near(row + col + both)
            return carry

        lax.fori_loop(0, pm // 256, body, 0)
        both = dot(tailp[...], feats, NT)
        real = lax.broadcasted_iota(jnp.int32, both.shape, 0) < n_pool - pm
        kt[pm : pm + 16, cols] = jnp.where(real, near(row + cs_tail + both), 0.0).astype(BF16)
        predv[:, cols] = dot(coefp[...], kt[:, cols], NN)

    core_sent = {}
    quart_sent = {}

    def lane_of(s):
        return slice(PLACE[s] * lanes, (PLACE[s] + 1) * lanes)

    def share(slots):
        if zs:
            for s in slots:
                psend[PLACE[s]] = predv[half_at(1 - c), lane_of(s)].astype(BF16)
                core_sent[s] = send(psend.at[PLACE[s]], precv.at[PLACE[s]], partner)

    def spread(slots):
        if not zs:
            return
        for s in slots:
            core_sent[s].wait_recv()
            predv[half_at(c), lane_of(s)] += precv[PLACE[s]].astype(F32)
            back = PLACE[(RING - s) % RING]
            for k, xd in ((0, x), (1, 1 - x)):
                if s == 0 and k == 0:
                    continue
                qsend[PLACE[s], k] = predv[quart_at(c * 2 + xd), lane_of(s)].astype(BF16)
                quart_sent[s, k] = send(
                    qsend.at[PLACE[s], k], qrecv.at[back, k], at(z + s, xd, c)
                )

    ready((0,))
    kernel_of(0, 1)
    share((0,))
    forward(2)
    ready((1, 7))
    kernel_of(PLACE[1], 2)
    share((1, 7))
    spread((0,))
    forward(3)
    ready((2, 6))
    kernel_of(PLACE[2], 2)
    share((2, 6))
    spread((1, 7))
    forward(4)
    ready((3, 5))
    kernel_of(PLACE[3], 2)
    share((3, 5))
    spread((2, 6))
    ready((4,))
    kernel_of(1, 1)
    share((4,))
    spread((3, 5))
    if zs:
        for copy in tg_sent:
            copy.wait_recv()
    tt[...] = tg[...].T
    spread((4,))

    total = predv[quart_at(j), lane_of(0)]
    for s in (0, 1, 7, 2, 6, 3, 5, 4):
        for k in (0, 1):
            if (s, k) in quart_sent:
                quart_sent[s, k].wait_recv()
                total = total + qrecv[PLACE[(RING - s) % RING], k].astype(F32)
    mine_now = total - tt[quart_at(j), :]
    res[0, quart_at(j), :] = mine_now.astype(BF16)
    rq[quart_at(j), :] = mine_now
    if zs:
        quarter = res.at[0, quart_at(j)]
        res_x = send(quarter, quarter, facing)
        far = (4, 3, 5, 2, 6, 1, 7)
        res_z = {}
        for s in far:
            res_z[s, 0] = send(
                quarter, res.at[PLACE[(RING - s) % RING], quart_at(j)], at(z + s, x, c)
            )
        res_x.wait_recv()
        other = res.at[0, quart_at(jx)]
        for s in far:
            res_z[s, 1] = send(
                other, res.at[PLACE[(RING - s) % RING], quart_at(jx)], at(z + s, x, c)
            )
        res_mate = {}
        block = res.at[0, half_at(c)]
        res_mate[0] = send(block, block, partner)
        wide_q = rq.at[quart_at(j)]
        rq_sent = [send(wide_q, wide_q, dev) for dev in (partner, facing, across)]
        for s in (1, 7, 2, 6, 3, 5, 4):
            back = (RING - s) % RING
            res_z[back, 0].wait_recv()
            res_z[back, 1].wait_recv()
            block = res.at[PLACE[s], half_at(c)]
            res_mate[s] = send(block, block, partner)

    def res_ready(slots):
        if zs:
            for s in slots:
                res_mate[s].wait_recv()

    def gradient(p0, n, first):
        cols = slice(p0 * lanes, (p0 + n) * lanes)
        left = jnp.concatenate([res[p, 0:og, :] for p in range(p0, p0 + n)], axis=1)

        def part(n0, width):
            n0 = pl.multiple_of(n0, 128)
            term = dot(left, kt[pl.ds(n0, width), cols], NT)
            if first:
                gp[:, pl.ds(n0, width)] = term
            else:
                gpb[:, pl.ds(n0, width)] = (gp[:, pl.ds(n0, width)] + term).astype(BF16)

        def body(m, carry):
            part(m * 256, 256)
            return carry

        lax.fori_loop(0, pm // 256, body, 0)
        part(pm, pp - pm)

    res_ready((1, 7, 2, 6, 3, 5))
    gradient(2, 6, True)
    res_ready((4, 0))
    gradient(0, 2, False)

    def own_term(s, h):
        col = lax.rem(y + s + RING, RING) * chunk + h * sub
        return dot(gpb[...], oht[:, pl.ds(pl.multiple_of(col, 128), sub)], NN)

    if ys:
        chain = {}
        for t in range(1, 5):
            s = 5 - t
            for h in (0, 1):
                terms = {1: own_term(s, h)}
                terms[-1] = terms[1] if t == 1 else own_term(-s, h)
                for w, way in enumerate((1, -1)):
                    first = slice(0, cut) if way == 1 else slice(cut, og)
                    if t == 1:
                        ysend[w, 0, h, first, :] = terms[way][first].astype(BF16)
                        chain[way, t, h] = send(
                            ysend.at[w, 0, h, first], yrecv.at[w, 0, h, first], at_y(y + way, xl)
                        )
                        continue
                    chain[way, t - 1, h].wait_recv()
                    if t == 2:
                        rest = slice(cut, og) if way == 1 else slice(0, cut)
                        ysend[w, 1, h, first, :] = (
                            terms[way][first] + yrecv[w, 0, h, first, :].astype(F32)
                        ).astype(BF16)
                        ysend[w, 1, h, rest, :] = terms[way][rest].astype(BF16)
                    else:
                        ysend[w, t - 1, h] = (
                            terms[way] + yrecv[w, t - 2, h].astype(F32)
                        ).astype(BF16)
                    chain[way, t, h] = send(
                        ysend.at[w, t - 1, h], yrecv.at[w, t - 1, h], at_y(y + way, xl)
                    )
        for h in (0, 1):
            fin[h] = own_term(0, h)
        for h in (0, 1):
            chain[1, 4, h].wait_recv()
            chain[-1, 4, h].wait_recv()
            fin[h] = fin[h] + yrecv[0, 3, h].astype(F32) + yrecv[1, 3, h].astype(F32)
        xsend[...] = fin[1 - xl].astype(BF16)
        swap = send(xsend, xrecv, at_y(y, 1 - xl))
        swap.wait_recv()
        grad[0, xl] = (fin[xl] + xrecv[...].astype(F32)).astype(BF16)
        own = grad.at[0, xl]
        back = {}
        for way, slot in ((1, RING - 1), (-1, 1)):
            back[way, 1, 0] = send(own, grad.at[slot, xl], at_y(y + way, xl))
        cross_l = send(own, own, at_y(y, 1 - xl))
    else:
        for s in range(RING):
            for h in (0, 1):
                grad[s, h] = own_term(s, h).astype(BF16)

    stores = []

    def store(s, h):
        col = lax.rem(y + s, RING) * chunk + h * sub
        copy = pltpu.make_async_copy(
            grad.at[s, h],
            grad_out.at[:, pl.ds(pl.multiple_of(col, 128), sub)],
            osem.at[len(stores)],
        )
        copy.start()
        stores.append(copy)

    if ys:
        store(0, xl)
        cross_l.wait_recv()
        other = grad.at[0, 1 - xl]
        for way, slot in ((1, RING - 1), (-1, 1)):
            back[way, 1, 1] = send(other, grad.at[slot, 1 - xl], at_y(y + way, xl))
        store(0, 1 - xl)
        for level in range(1, 5):
            for stream, h in ((0, xl), (1, 1 - xl)):
                for way in (1, -1):
                    straight = (way == 1) == (stream == 0)
                    if level == 4 and not straight:
                        continue
                    back[way, level, stream].wait_recv()
                    slot = slot_of(way, level)
                    if level < 3 or (level == 3 and straight):
                        back[way, level + 1, stream] = send(
                            grad.at[slot, h], grad.at[slot_of(way, level + 1), h],
                            at_y(y + way, xl),
                        )
                    store(slot, h)
                    if level == 1 and stream == 0 and way == 1 and zs:
                        for copy in rq_sent:
                            copy.wait_recv()
                        rt[...] = rq[...].T
                        res_out[...] = rt[rows_at(j), 0:out]
    else:
        for s in range(RING):
            for h in (0, 1):
                store(s, h)
        if zs:
            for copy in rq_sent:
                copy.wait_recv()
        rt[...] = rq[...].T
        res_out[...] = rt[rows_at(j), 0:out]
    for copy in stores:
        copy.wait()
    for copy in started:
        copy.wait_send()


def on_device(zs, ys, bpool, bidx, cpool, cidx, tgt, coef):
    rows, d = bidx.shape[0], bpool.shape[1]
    out, cen = tgt.shape[1], cidx.shape[0]
    n_pool = cpool.shape[0]
    outp, og = up(out, 64), up(out, 16)
    pp = n_pool // 256 * 256 + 128
    lanes = 4 * rows
    half, quart = outp // 2, outp // 4
    wide = up(outp, 128)
    chunk = cen // RING
    sub = chunk // 2
    vmem = pl.BlockSpec(memory_space=pltpu.VMEM)
    hbm = pl.BlockSpec(memory_space=pl.ANY)
    grad, residual = pl.pallas_call(
        functools.partial(step_kernel, zs, ys),
        out_shape=(
            jax.ShapeDtypeStruct((og, cen), BF16),
            jax.ShapeDtypeStruct((rows, out), F32),
        ),
        in_specs=[vmem, vmem, vmem, hbm, vmem, hbm],
        out_specs=(hbm, vmem),
        scratch_shapes=[
            pltpu.VMEM((up(bpool.shape[0], 16), d), BF16),
            pltpu.VMEM((RING, lanes, d), BF16),
            pltpu.VMEM((n_pool, d), BF16),
            pltpu.VMEM((16, d), BF16),
            pltpu.VMEM((pp, 128), F32),
            pltpu.VMEM((pp, cen), BF16),
            pltpu.VMEM((out, cen), F32),
            pltpu.VMEM((og, cen), BF16),
            pltpu.VMEM((outp, pp), BF16),
            pltpu.VMEM((pp, RING * lanes), BF16),
            pltpu.VMEM((outp, RING * lanes), F32),
            pltpu.VMEM((RING, half, lanes), BF16),
            pltpu.VMEM((RING, half, lanes), BF16),
            pltpu.VMEM((RING, 2, quart, lanes), BF16),
            pltpu.VMEM((RING, 2, quart, lanes), BF16),
            pltpu.VMEM((lanes, wide), F32),
            pltpu.VMEM((wide, lanes), F32),
            pltpu.VMEM((RING, outp, lanes), BF16),
            pltpu.VMEM((outp, lanes), F32),
            pltpu.VMEM((lanes, outp), F32),
            pltpu.VMEM((og, pp), F32),
            pltpu.VMEM((og, pp), BF16),
            pltpu.VMEM((2, 4, 2, og, sub), BF16),
            pltpu.VMEM((2, 4, 2, og, sub), BF16),
            pltpu.VMEM((2, og, sub), F32),
            pltpu.VMEM((og, sub), BF16),
            pltpu.VMEM((og, sub), BF16),
            pltpu.VMEM((RING, 2, og, sub), BF16),
            pltpu.SemaphoreType.DMA((COPIES,)),
            pltpu.SemaphoreType.DMA((COPIES,)),
            pltpu.SemaphoreType.DMA((2,)),
            pltpu.SemaphoreType.DMA((2 * RING,)),
        ],
        compiler_params=pltpu.CompilerParams(
            collective_id=0, has_side_effects=True, vmem_limit_bytes=62 * 1024 * 1024
        ),
        name="regression_step",
    )(
        bidx.reshape(1, rows), bpool, cidx.reshape(1, cen), cpool, tgt, coef.T,
    )
    batch_total = rows * lax.axis_size("batch") * lax.axis_size("centre")
    step_size = 8.0 / math.sqrt(batch_total)
    updated = coef - step_size * grad[:out].astype(F32).T
    return updated, residual


def solution(mesh):
    both = ("batch", "centre")
    zs, ys = mesh.shape["centre"] > 1, mesh.shape["batch"] > 1
    return jax.shard_map(
        functools.partial(on_device, zs, ys),
        mesh=mesh,
        in_specs=(
            P(both, None), P(both), P("centre", None), P("centre"), P(both, None), P("centre", None),
        ),
        out_specs=(P("centre", None), P(both, None)),
        check_vma=False,
    )
```

```python
import functools
import math

import jax
import jax.numpy as jnp
from jax import lax
from jax.experimental import pallas as pl
from jax.experimental.pallas import tpu as pltpu
from jax.sharding import PartitionSpec as P

MESH = pl.DeviceIdType.MESH
F32 = jnp.float32
BF16 = jnp.bfloat16
RING = 8
NT = (((1,), (1,)), ((), ()))
NN = (((1,), (0,)), ((), ()))
TN = (((0,), (0,)), ((), ()))
PLACE = (0, 1, 3, 5, 7, 6, 4, 2)
COPIES = 128
LOG2E = 1.4426950408889634


def up(n, k):
    return -(-n // k) * k


def dot(a, b, dims):
    return lax.dot_general(a, b, dims, preferred_element_type=F32)


def step_kernel(*refs):
    inner_kernel([], *refs)


def inner_kernel(
    started, zs, ys, bidx, bpool, cidx, cpool, ctail, tgt, coef, grad_out, res_out,
    bsel, xall, pool, cs, oht, coefv, coefb, coefp, kt, predv, psend, precv,
    qsend, qrecv, tg, tt, res, rq, rt, gp, gpb, ysend, yrecv, fin, xsend, xrecv, grad,
    ssem, rsem, lsem, osem,
):
    bi = lax.axis_index("batch")
    ci = lax.axis_index("centre")
    y, xl = bi // 2, bi % 2
    z, x, c = ci // 4, (ci // 2) % 2, ci % 2
    rows, d = tgt.shape[0], bpool.shape[1]
    out = tgt.shape[1]
    cen = cidx.shape[1]
    n_pool = cpool.shape[0]
    pp = kt.shape[0]
    pm = n_pool // 256 * 256
    full = pool.shape[0]
    tall = full // 5 if full % 80 == 0 else full // 2 // 16 * 16 if full % 32 == 0 else 16
    lanes = 4 * rows
    half, quart = predv.shape[0] // 2, predv.shape[0] // 4
    og = gp.shape[0]
    cut = up(og // 2, 16)
    chunk = cen // RING
    sub = chunk // 2

    def at(z_, x_, c_):
        return (bi, lax.rem(z_ + 2 * RING, RING) * 4 + x_ * 2 + c_)

    def at_y(y_, xl_):
        return (lax.rem(y_ + 2 * RING, RING) * 2 + xl_, ci)

    count = [0]
    def send(src, dst, dev):
        n = count[0]
        count[0] += 1
        copy = pltpu.make_async_remote_copy(
            src_ref=src, dst_ref=dst, send_sem=ssem.at[n], recv_sem=rsem.at[n],
            device_id=dev, device_id_type=MESH,
        )
        copy.start()
        started.append(copy)
        return copy

    partner = at(z, x, 1 - c)
    facing = at(z, 1 - x, c)
    across = at(z, 1 - x, 1 - c)
    greet = []
    if zs:
        greet += [partner, facing, across]
        greet += [at(z + s, x, c) for s in range(1, RING)]
        greet += [at(z + s, 1 - x, c) for s in range(1, RING)]
    if ys:
        greet += [at_y(y + 1, xl), at_y(y - 1, xl), at_y(y, 1 - xl)]
    barrier = pltpu.get_barrier_semaphore()
    for dev in greet:
        pl.semaphore_signal(barrier, inc=1, device_id=dev, device_id_type=MESH)

    load_pool = pltpu.make_async_copy(cpool.at[0:pm], pool.at[0:pm], lsem.at[0])
    load_pool.start()
    load_coef = pltpu.make_async_copy(coef, coefv, lsem.at[1])
    load_coef.start()

    def over(n, body):
        times = 3 if n % 3 == 0 else 1

        def group(m, carry):
            for k in range(times):
                body((m * times + k) * 256)
            return carry

        lax.fori_loop(0, n // times, group, 0)

    def rows_at(k):
        return pl.ds(pl.multiple_of(k * rows, rows), rows)

    def quart_at(k):
        return pl.ds(pl.multiple_of(k * quart, 16), quart)

    def half_at(k):
        return pl.ds(pl.multiple_of(k * half, 16), half)

    j = c * 2 + x
    jx = c * 2 + 1 - x

    bsel[...] = jnp.zeros_like(bsel)
    bsel[0 : bpool.shape[0], :] = bpool[...]
    base = (bi * lax.axis_size("centre") + ci) * bpool.shape[0]
    place = lax.broadcasted_iota(jnp.int32, (bsel.shape[0], rows), 0) + base
    pick = jnp.where(place == bidx[...], -2.0, 0.0).astype(BF16)
    xall[0, rows_at(j), :] = dot(pick, bsel[...], TN).astype(BF16)
    tg[rows_at(j), :] = jnp.zeros((rows, tg.shape[1]), F32)
    tg[rows_at(j), 0:out] = tgt[...]

    cbase = ci * n_pool
    step_rows = 32

    def build(m, carry):
        r0 = pl.multiple_of(m * step_rows, step_rows)
        at_row = lax.broadcasted_iota(jnp.int32, (step_rows, cen), 0) + (cbase + r0)
        oht[pl.ds(r0, step_rows), :] = jnp.where(at_row == cidx[...], 1.0, 0.0).astype(BF16)
        return carry

    lax.fori_loop(0, pp // step_rows, build, 0)

    pl.semaphore_wait(barrier, len(greet))

    ring = {}
    mate = {}
    if zs:
        own = xall.at[0, rows_at(j)]
        cross_x = send(own, own, facing)
        for way, slot in ((1, RING - 1), (-1, 1)):
            ring[way, 1, 0] = send(own, xall.at[PLACE[slot], rows_at(j)], at(z + way, x, c))
        mate[0, 0] = send(own, own, partner)
        mine = tg.at[rows_at(j)]
        tg_sent = [send(mine, mine, dev) for dev in (partner, facing, across)]

    def slot_of(way, level):
        return RING - level if way == 1 else level

    def forward(level):
        if not zs:
            return
        for stream, place_of in ((0, j), (1, jx)):
            for way in (1, -1):
                if level == 0:
                    if way == 1:
                        if stream == 0:
                            continue
                        cross_x.wait_recv()
                        block = xall.at[0, rows_at(jx)]
                        mate[0, 1] = send(block, block, partner)
                    elif stream == 0:
                        continue
                else:
                    if level == 4 and (way == 1) != (stream == 0):
                        continue
                    ring[way, level, stream].wait_recv()
                slot = slot_of(way, level) % RING
                block = xall.at[PLACE[slot], rows_at(place_of)]
                if level < 4 and (level < 3 or (way == 1) == (stream == 0)):
                    nxt = slot_of(way, level + 1)
                    ring[way, level + 1, stream] = send(
                        block, xall.at[PLACE[nxt], rows_at(place_of)], at(z + way, x, c)
                    )
                if level:
                    mate[slot, stream] = send(block, block, partner)

    def ready(slots):
        if zs:
            for s in slots:
                mate[s, 0].wait_recv()
                mate[s, 1].wait_recv()

    load_pool.wait()
    last = ctail[...]
    real = lax.broadcasted_iota(jnp.int32, last.shape, 0) < n_pool - pm
    pool[pm:full, :] = jnp.where(real, last, jnp.zeros_like(last))

    def squares(r0, n):
        wide = pool[pl.ds(r0, n), :].astype(F32)
        cs[pl.ds(r0, n), :] = jnp.broadcast_to(
            jnp.sum(wide * wide, axis=1, keepdims=True), (n, 128)
        )

    over(pm // 256, lambda r0: squares(pl.multiple_of(r0, 256), 256))
    squares(pm, full - pm)
    kt[full:, :] = jnp.zeros_like(kt[full:, :])
    forward(0)

    load_coef.wait()
    coefb[...] = jnp.zeros_like(coefb)
    coefb[0:out, :] = coefv[...].astype(BF16)
    if og < coefp.shape[0]:
        coefp[og:, :] = jnp.zeros_like(coefp[og:, :])

    def permute(n, width):
        n = pl.multiple_of(n, 128)
        coefp[0:og, pl.ds(n, width)] = dot(
            coefb[...], oht[pl.ds(n, width), :], NT
        ).astype(BF16)

    def near(squared):
        floor = jnp.maximum(squared, 1e-30)
        return jnp.exp2(floor * lax.rsqrt(floor) * -LOG2E).astype(BF16)

    def kernel_of(p0, n):
        width = n * lanes
        cols = slice(p0 * lanes, p0 * lanes + width)
        feats = xall[p0 : p0 + n].reshape(width, d)
        wide = feats.astype(F32)
        size = jnp.sum(wide * wide, axis=1, keepdims=True) * 0.25
        row = jnp.broadcast_to(size, (width, 128)).T[0:1, :]

        def body(m, carry):
            r0 = pl.multiple_of(m * tall, 16)
            both = dot(pool[pl.ds(r0, tall), :], xall[p0 : p0 + n].reshape(width, d), NT)
            col = cs[pl.ds(r0, tall), :]
            col = jnp.concatenate([col] * (width // 128), axis=1) if width > 128 else col[:, :width]
            kt[pl.ds(r0, tall), cols] = near(row + col + both)
            return carry

        for m in range(full // tall):
            body(m, 0)
        predv[:, cols] = dot(coefp[...], kt[:, cols], NN)

    core_sent = {}
    quart_sent = {}

    def lane_of(s):
        return slice(PLACE[s] * lanes, (PLACE[s] + 1) * lanes)

    def share(slots):
        if zs:
            for s in slots:
                psend[PLACE[s]] = predv[half_at(1 - c), lane_of(s)].astype(BF16)
                core_sent[s] = send(psend.at[PLACE[s]], precv.at[PLACE[s]], partner)

    def spread(slots):
        if not zs:
            return
        for s in slots:
            core_sent[s].wait_recv()
            predv[half_at(c), lane_of(s)] += precv[PLACE[s]].astype(F32)
            back = PLACE[(RING - s) % RING]
            for k, xd in ((0, x), (1, 1 - x)):
                if s == 0 and k == 0:
                    continue
                qsend[PLACE[s], k] = predv[quart_at(c * 2 + xd), lane_of(s)].astype(BF16)
                quart_sent[s, k] = send(
                    qsend.at[PLACE[s], k], qrecv.at[back, k], at(z + s, xd, c)
                )

    cuts = (0, pm // 768 * 512, pm) if pm % 768 == 0 else (0, 0, pm)
    over((cuts[1] - cuts[0]) // 256, lambda n0: permute(n0, 256))
    forward(1)
    over((cuts[2] - cuts[1]) // 256, lambda n0: permute(cuts[1] + n0, 256))
    permute(pm, pp - pm)
    ready((0, 1))
    kernel_of(0, 2)
    share((0, 1))
    forward(2)
    ready((7, 2))
    kernel_of(2, 2)
    share((7, 2))
    spread((0, 1))
    forward(3)
    ready((6, 3))
    kernel_of(4, 2)
    share((6, 3))
    spread((7, 2))
    forward(4)
    ready((5, 4))
    kernel_of(6, 2)
    share((5, 4))
    spread((6, 3))
    if zs:
        for copy in tg_sent:
            copy.wait_recv()
    tt[...] = tg[...].T
    spread((5, 4))

    total = predv[quart_at(j), lane_of(0)]
    for s in (0, 1, 7, 2, 6, 3, 5, 4):
        for k in (0, 1):
            if (s, k) in quart_sent:
                quart_sent[s, k].wait_recv()
                total = total + qrecv[PLACE[(RING - s) % RING], k].astype(F32)
    mine_now = total - tt[quart_at(j), :]
    res[0, quart_at(j), :] = mine_now.astype(BF16)
    rq[quart_at(j), :] = mine_now
    if zs:
        quarter = res.at[0, quart_at(j)]
        res_x = send(quarter, quarter, facing)
        far = (4, 3, 5, 2, 6, 1, 7)
        res_z = {}
        for s in far:
            res_z[s, 0] = send(
                quarter, res.at[PLACE[(RING - s) % RING], quart_at(j)], at(z + s, x, c)
            )
        res_x.wait_recv()
        other = res.at[0, quart_at(jx)]
        for s in far:
            res_z[s, 1] = send(
                other, res.at[PLACE[(RING - s) % RING], quart_at(jx)], at(z + s, x, c)
            )
        res_mate = {}
        block = res.at[0, half_at(c)]
        res_mate[0] = send(block, block, partner)
        wide_q = rq.at[quart_at(j)]
        rq_sent = [send(wide_q, wide_q, dev) for dev in (partner, facing, across)]
        for s in (1, 7, 2, 6, 3, 5, 4):
            back = (RING - s) % RING
            res_z[back, 0].wait_recv()
            res_z[back, 1].wait_recv()
            block = res.at[PLACE[s], half_at(c)]
            res_mate[s] = send(block, block, partner)

    def res_ready(slots):
        if zs:
            for s in slots:
                res_mate[s].wait_recv()

    def gradient(p0, n, first):
        cols = slice(p0 * lanes, (p0 + n) * lanes)
        left = jnp.concatenate([res[p, 0:og, :] for p in range(p0, p0 + n)], axis=1)

        def part(n0, width):
            n0 = pl.multiple_of(n0, 128)
            term = dot(left, kt[pl.ds(n0, width), cols], NT)
            if first:
                gp[:, pl.ds(n0, width)] = term
            else:
                gpb[:, pl.ds(n0, width)] = (gp[:, pl.ds(n0, width)] + term).astype(BF16)

        over(pm // 256, lambda n0: part(n0, 256))
        part(pm, pp - pm)

    res_ready((0, 1, 7, 2, 6, 3))
    gradient(0, 6, True)
    res_ready((5, 4))
    gradient(6, 2, False)

    def own_term(s):
        col = lax.rem(y + s + RING, RING) * chunk
        return dot(gpb[...], oht[:, pl.ds(pl.multiple_of(col, 128), chunk)], NN)

    if ys:
        chain = {}
        for t in range(1, 5):
            s = 5 - t
            own_terms = {1: own_term(s)}
            own_terms[-1] = own_terms[1] if t == 1 else own_term(-s)
            for h in (0, 1):
                terms = {way: own_terms[way][:, h * sub : (h + 1) * sub] for way in (1, -1)}
                for w, way in enumerate((1, -1)):
                    first = slice(0, cut) if way == 1 else slice(cut, og)
                    if t == 1:
                        ysend[w, 0, h, first, :] = terms[way][first].astype(BF16)
                        chain[way, t, h] = send(
                            ysend.at[w, 0, h, first], yrecv.at[w, 0, h, first], at_y(y + way, xl)
                        )
                        continue
                    chain[way, t - 1, h].wait_recv()
                    if t == 2:
                        rest = slice(cut, og) if way == 1 else slice(0, cut)
                        ysend[w, 1, h, first, :] = (
                            terms[way][first] + yrecv[w, 0, h, first, :].astype(F32)
                        ).astype(BF16)
                        ysend[w, 1, h, rest, :] = terms[way][rest].astype(BF16)
                    else:
                        ysend[w, t - 1, h] = (
                            terms[way] + yrecv[w, t - 2, h].astype(F32)
                        ).astype(BF16)
                    chain[way, t, h] = send(
                        ysend.at[w, t - 1, h], yrecv.at[w, t - 1, h], at_y(y + way, xl)
                    )
        own_here = own_term(0)
        for h in (0, 1):
            fin[h] = own_here[:, h * sub : (h + 1) * sub]
        for h in (0, 1):
            chain[1, 4, h].wait_recv()
            chain[-1, 4, h].wait_recv()
            fin[h] = fin[h] + yrecv[0, 3, h].astype(F32) + yrecv[1, 3, h].astype(F32)
        xsend[...] = fin[1 - xl].astype(BF16)
        swap = send(xsend, xrecv, at_y(y, 1 - xl))
        swap.wait_recv()
        grad[0, xl] = (fin[xl] + xrecv[...].astype(F32)).astype(BF16)
        own = grad.at[0, xl]
        back = {}
        for way, slot in ((1, RING - 1), (-1, 1)):
            back[way, 1, 0] = send(own, grad.at[slot, xl], at_y(y + way, xl))
        cross_l = send(own, own, at_y(y, 1 - xl))
    else:
        for s in range(RING):
            for h in (0, 1):
                grad[s, h] = own_term(s)[:, h * sub : (h + 1) * sub].astype(BF16)

    stores = []

    def store(s, h):
        col = lax.rem(y + s, RING) * chunk + h * sub
        copy = pltpu.make_async_copy(
            grad.at[s, h],
            grad_out.at[:, pl.ds(pl.multiple_of(col, 128), sub)],
            osem.at[len(stores)],
        )
        copy.start()
        stores.append(copy)

    if ys:
        store(0, xl)
        cross_l.wait_recv()
        other = grad.at[0, 1 - xl]
        for way, slot in ((1, RING - 1), (-1, 1)):
            back[way, 1, 1] = send(other, grad.at[slot, 1 - xl], at_y(y + way, xl))
        store(0, 1 - xl)
        for level in range(1, 5):
            for stream, h in ((0, xl), (1, 1 - xl)):
                for way in (1, -1):
                    straight = (way == 1) == (stream == 0)
                    if level == 4 and not straight:
                        continue
                    back[way, level, stream].wait_recv()
                    slot = slot_of(way, level)
                    if level < 3 or (level == 3 and straight):
                        back[way, level + 1, stream] = send(
                            grad.at[slot, h], grad.at[slot_of(way, level + 1), h],
                            at_y(y + way, xl),
                        )
                    store(slot, h)
                    if level == 1 and stream == 0 and way == 1 and zs:
                        for copy in rq_sent:
                            copy.wait_recv()
                        rt[...] = rq[...].T
                        res_out[...] = rt[rows_at(j), 0:out]
    else:
        for s in range(RING):
            for h in (0, 1):
                store(s, h)
        if zs:
            for copy in rq_sent:
                copy.wait_recv()
        rt[...] = rq[...].T
        res_out[...] = rt[rows_at(j), 0:out]
    for copy in stores:
        copy.wait()
    for copy in started:
        copy.wait_send()


def on_device(zs, ys, bpool, bidx, cpool, cidx, tgt, coef):
    rows, d = bidx.shape[0], bpool.shape[1]
    out, cen = tgt.shape[1], cidx.shape[0]
    n_pool = cpool.shape[0]
    outp, og = up(out, 64), up(out, 16)
    pp = n_pool // 256 * 256 + 128
    lanes = 4 * rows
    half, quart = outp // 2, outp // 4
    wide = up(outp, 128)
    chunk = cen // RING
    sub = chunk // 2
    vmem = pl.BlockSpec(memory_space=pltpu.VMEM)
    hbm = pl.BlockSpec(memory_space=pl.ANY)
    tail = pl.BlockSpec((16, d), lambda i: (n_pool // 256 * 16, 0))
    grad, residual = pl.pallas_call(
        functools.partial(step_kernel, zs, ys),
        out_shape=(
            jax.ShapeDtypeStruct((og, cen), BF16),
            jax.ShapeDtypeStruct((rows, out), F32),
        ),
        grid=(1,),
        in_specs=[vmem, vmem, vmem, hbm, tail, vmem, hbm],
        out_specs=(hbm, vmem),
        scratch_shapes=[
            pltpu.VMEM((up(bpool.shape[0], 16), d), BF16),
            pltpu.VMEM((RING, lanes, d), BF16),
            pltpu.VMEM((up(n_pool, 16), d), BF16),
            pltpu.VMEM((pp, 128), F32),
            pltpu.VMEM((pp, cen), BF16),
            pltpu.VMEM((out, cen), F32),
            pltpu.VMEM((og, cen), BF16),
            pltpu.VMEM((outp, pp), BF16),
            pltpu.VMEM((pp, RING * lanes), BF16),
            pltpu.VMEM((outp, RING * lanes), F32),
            pltpu.VMEM((RING, half, lanes), BF16),
            pltpu.VMEM((RING, half, lanes), BF16),
            pltpu.VMEM((RING, 2, quart, lanes), BF16),
            pltpu.VMEM((RING, 2, quart, lanes), BF16),
            pltpu.VMEM((lanes, wide), F32),
            pltpu.VMEM((wide, lanes), F32),
            pltpu.VMEM((RING, outp, lanes), BF16),
            pltpu.VMEM((outp, lanes), F32),
            pltpu.VMEM((lanes, outp), F32),
            pltpu.VMEM((og, pp), F32),
            pltpu.VMEM((og, pp), BF16),
            pltpu.VMEM((2, 4, 2, og, sub), BF16),
            pltpu.VMEM((2, 4, 2, og, sub), BF16),
            pltpu.VMEM((2, og, sub), F32),
            pltpu.VMEM((og, sub), BF16),
            pltpu.VMEM((og, sub), BF16),
            pltpu.VMEM((RING, 2, og, sub), BF16),
            pltpu.SemaphoreType.DMA((COPIES,)),
            pltpu.SemaphoreType.DMA((COPIES,)),
            pltpu.SemaphoreType.DMA((2,)),
            pltpu.SemaphoreType.DMA((2 * RING,)),
        ],
        compiler_params=pltpu.CompilerParams(
            collective_id=0, has_side_effects=True, vmem_limit_bytes=62 * 1024 * 1024
        ),
        name="regression_step",
    )(
        bidx.reshape(1, rows), bpool, cidx.reshape(1, cen), cpool, cpool, tgt, coef.T,
    )
    batch_total = rows * lax.axis_size("batch") * lax.axis_size("centre")
    step_size = 8.0 / math.sqrt(batch_total)
    updated = coef - step_size * grad[:out].astype(F32).T
    return updated, residual


def solution(mesh):
    both = ("batch", "centre")
    zs, ys = mesh.shape["centre"] > 1, mesh.shape["batch"] > 1
    return jax.shard_map(
        functools.partial(on_device, zs, ys),
        mesh=mesh,
        in_specs=(
            P(both, None), P(both), P("centre", None), P("centre"), P(both, None), P("centre", None),
        ),
        out_specs=(P("centre", None), P(both, None)),
        check_vma=False,
    )
```

```python
import functools
import math

import jax
import jax.numpy as jnp
from jax import lax
from jax.experimental import pallas as pl
from jax.experimental.pallas import tpu as pltpu
from jax.sharding import PartitionSpec as P

MESH = pl.DeviceIdType.MESH
F32 = jnp.float32
BF16 = jnp.bfloat16
RING = 8
NT = (((1,), (1,)), ((), ()))
NN = (((1,), (0,)), ((), ()))
TN = (((0,), (0,)), ((), ()))
PLACE = (0, 1, 3, 5, 7, 6, 4, 2)
COPIES = 176
LOG2E = 1.4426950408889634


def up(n, k):
    return -(-n // k) * k


def dot(a, b, dims):
    return lax.dot_general(a, b, dims, preferred_element_type=F32)


def step_kernel(*refs):
    inner_kernel([], *refs)


def inner_kernel(
    started, zs, ys, bidx, bpool, cidx, cpool, ctail, tgt, coef, grad_out, res_out,
    bsel, xall, pool, cs, oht, coefv, coefb, coefp, kt, predv, psend, precv,
    qsend, qrecv, tg, tt, res, rq, rt, gp, gpb, terms, xps, xpr, yps, ypr, yqs, yqr, xsend, xrecv, grad,
    ssem, rsem, lsem, osem,
):
    bi = lax.axis_index("batch")
    ci = lax.axis_index("centre")
    y, xl = bi // 2, bi % 2
    z, x, c = ci // 4, (ci // 2) % 2, ci % 2
    rows, d = tgt.shape[0], bpool.shape[1]
    out = tgt.shape[1]
    cen = cidx.shape[1]
    n_pool = cpool.shape[0]
    pp = kt.shape[0]
    pm = n_pool // 256 * 256
    full = pool.shape[0]
    tall = full // 5 if full % 80 == 0 else full // 2 // 16 * 16 if full % 32 == 0 else 16
    lanes = 4 * rows
    half, quart = predv.shape[0] // 2, predv.shape[0] // 4
    og = gp.shape[0]
    top = xps.shape[1]
    mid_p = up(top // 2, 16)
    mid_q = top + up((og - top) // 2, 16)
    split = up((og + og - top) // 2, 16)
    chunk = cen // RING
    sub = chunk // 2

    def at(z_, x_, c_):
        return (bi, lax.rem(z_ + 2 * RING, RING) * 4 + x_ * 2 + c_)

    def at_y(y_, xl_):
        return (lax.rem(y_ + 2 * RING, RING) * 2 + xl_, ci)

    count = [0]
    def send(src, dst, dev):
        n = count[0]
        count[0] += 1
        copy = pltpu.make_async_remote_copy(
            src_ref=src, dst_ref=dst, send_sem=ssem.at[n], recv_sem=rsem.at[n],
            device_id=dev, device_id_type=MESH,
        )
        copy.start()
        started.append(copy)
        return copy

    partner = at(z, x, 1 - c)
    facing = at(z, 1 - x, c)
    across = at(z, 1 - x, 1 - c)
    greet = []
    if zs:
        greet += [partner, facing, across]
        greet += [at(z + s, x, c) for s in range(1, RING)]
        greet += [at(z + s, 1 - x, c) for s in range(1, RING)]
    if ys:
        greet += [at_y(y + 1, xl), at_y(y - 1, xl), at_y(y, 1 - xl)]
    barrier = pltpu.get_barrier_semaphore()
    for dev in greet:
        pl.semaphore_signal(barrier, inc=1, device_id=dev, device_id_type=MESH)

    load_pool = pltpu.make_async_copy(cpool.at[0:pm], pool.at[0:pm], lsem.at[0])
    load_pool.start()
    load_coef = pltpu.make_async_copy(coef, coefv, lsem.at[1])
    load_coef.start()

    def over(n, body):
        times = 3 if n % 3 == 0 else 1

        def group(m, carry):
            for k in range(times):
                body((m * times + k) * 256)
            return carry

        lax.fori_loop(0, n // times, group, 0)

    def rows_at(k):
        return pl.ds(pl.multiple_of(k * rows, rows), rows)

    def quart_at(k):
        return pl.ds(pl.multiple_of(k * quart, 16), quart)

    def half_at(k):
        return pl.ds(pl.multiple_of(k * half, 16), half)

    j = c * 2 + x
    jx = c * 2 + 1 - x

    bsel[...] = jnp.zeros_like(bsel)
    bsel[0 : bpool.shape[0], :] = bpool[...]
    base = (bi * lax.axis_size("centre") + ci) * bpool.shape[0]
    place = lax.broadcasted_iota(jnp.int32, (bsel.shape[0], rows), 0) + base
    pick = jnp.where(place == bidx[...], -2.0, 0.0).astype(BF16)
    xall[0, rows_at(j), :] = dot(pick, bsel[...], TN).astype(BF16)
    tg[rows_at(j), :] = jnp.zeros((rows, tg.shape[1]), F32)
    tg[rows_at(j), 0:out] = tgt[...]

    cbase = ci * n_pool
    step_rows = 32

    def build(m, carry):
        r0 = pl.multiple_of(m * step_rows, step_rows)
        at_row = lax.broadcasted_iota(jnp.int32, (step_rows, cen), 0) + (cbase + r0)
        oht[pl.ds(r0, step_rows), :] = jnp.where(at_row == cidx[...], 1.0, 0.0).astype(BF16)
        return carry

    lax.fori_loop(0, pp // step_rows, build, 0)

    pl.semaphore_wait(barrier, len(greet))

    ring = {}
    mate = {}
    if zs:
        own = xall.at[0, rows_at(j)]
        cross_x = send(own, own, facing)
        for way, slot in ((1, RING - 1), (-1, 1)):
            ring[way, 1, 0] = send(own, xall.at[PLACE[slot], rows_at(j)], at(z + way, x, c))
        mate[0, 0] = send(own, own, partner)

    def slot_of(way, level):
        return RING - level if way == 1 else level

    def forward(level):
        if not zs:
            return
        for stream, place_of in ((0, j), (1, jx)):
            for way in (1, -1):
                if level == 0:
                    if way == 1:
                        if stream == 0:
                            continue
                        cross_x.wait_recv()
                        block = xall.at[0, rows_at(jx)]
                        mate[0, 1] = send(block, block, partner)
                    elif stream == 0:
                        continue
                else:
                    if level == 4 and (way == 1) != (stream == 0):
                        continue
                    ring[way, level, stream].wait_recv()
                slot = slot_of(way, level) % RING
                block = xall.at[PLACE[slot], rows_at(place_of)]
                if level < 4 and (level < 3 or (way == 1) == (stream == 0)):
                    nxt = slot_of(way, level + 1)
                    ring[way, level + 1, stream] = send(
                        block, xall.at[PLACE[nxt], rows_at(place_of)], at(z + way, x, c)
                    )
                if level:
                    mate[slot, stream] = send(block, block, partner)

    def ready(slots):
        if zs:
            for s in slots:
                mate[s, 0].wait_recv()
                mate[s, 1].wait_recv()

    load_pool.wait()
    last = ctail[...]
    real = lax.broadcasted_iota(jnp.int32, last.shape, 0) < n_pool - pm
    pool[pm:full, :] = jnp.where(real, last, jnp.zeros_like(last))

    def squares(r0, n):
        wide = pool[pl.ds(r0, n), :].astype(F32)
        cs[pl.ds(r0, n), :] = jnp.broadcast_to(
            jnp.sum(wide * wide, axis=1, keepdims=True), (n, 128)
        )

    over(pm // 256, lambda r0: squares(pl.multiple_of(r0, 256), 256))
    squares(pm, full - pm)
    kt[full:, :] = jnp.zeros_like(kt[full:, :])
    forward(0)

    load_coef.wait()
    coefb[...] = jnp.zeros_like(coefb)
    coefb[0:out, :] = coefv[...].astype(BF16)
    if og < coefp.shape[0]:
        coefp[og:, :] = jnp.zeros_like(coefp[og:, :])

    def permute(n, width):
        n = pl.multiple_of(n, 128)
        coefp[0:og, pl.ds(n, width)] = dot(
            coefb[...], oht[pl.ds(n, width), :], NT
        ).astype(BF16)

    def near(squared):
        floor = jnp.maximum(squared, 1e-30)
        return jnp.exp2(floor * lax.rsqrt(floor) * -LOG2E).astype(BF16)

    def kernel_of(p0, n):
        width = n * lanes
        cols = slice(p0 * lanes, p0 * lanes + width)
        feats = xall[p0 : p0 + n].reshape(width, d)
        wide = feats.astype(F32)
        size = jnp.sum(wide * wide, axis=1, keepdims=True) * 0.25
        row = jnp.broadcast_to(size, (width, 128)).T[0:1, :]

        def body(m, carry):
            r0 = pl.multiple_of(m * tall, 16)
            both = dot(pool[pl.ds(r0, tall), :], xall[p0 : p0 + n].reshape(width, d), NT)
            col = cs[pl.ds(r0, tall), :]
            col = jnp.concatenate([col] * (width // 128), axis=1) if width > 128 else col[:, :width]
            kt[pl.ds(r0, tall), cols] = near(row + col + both)
            return carry

        for m in range(full // tall):
            body(m, 0)
        predv[:, cols] = dot(coefp[...], kt[:, cols], NN)

    core_sent = {}
    quart_sent = {}

    def lane_of(s):
        return slice(PLACE[s] * lanes, (PLACE[s] + 1) * lanes)

    def share(slots):
        if zs:
            for s in slots:
                psend[PLACE[s]] = predv[half_at(1 - c), lane_of(s)].astype(BF16)
                core_sent[s] = send(psend.at[PLACE[s]], precv.at[PLACE[s]], partner)

    def spread(slots):
        if not zs:
            return
        for s in slots:
            core_sent[s].wait_recv()
            predv[half_at(c), lane_of(s)] += precv[PLACE[s]].astype(F32)
            back = PLACE[(RING - s) % RING]
            for k, xd in ((0, x), (1, 1 - x)):
                if s == 0 and k == 0:
                    continue
                qsend[PLACE[s], k] = predv[quart_at(c * 2 + xd), lane_of(s)].astype(BF16)
                quart_sent[s, k] = send(
                    qsend.at[PLACE[s], k], qrecv.at[back, k], at(z + s, xd, c)
                )

    cuts = (0, pm // 768 * 512, pm) if pm % 768 == 0 else (0, 0, pm)
    over((cuts[1] - cuts[0]) // 256, lambda n0: permute(n0, 256))
    forward(1)
    over((cuts[2] - cuts[1]) // 256, lambda n0: permute(cuts[1] + n0, 256))
    permute(pm, pp - pm)
    if zs:
        mine = tg.at[rows_at(j)]
        tg_sent = [send(mine, mine, dev) for dev in (partner, facing, across)]
    ready((0, 1))
    kernel_of(0, 2)
    share((0, 1))
    forward(2)
    ready((7, 2))
    kernel_of(2, 2)
    share((7, 2))
    spread((0, 1))
    forward(3)
    ready((6, 3))
    kernel_of(4, 2)
    share((6, 3))
    spread((7, 2))
    forward(4)
    ready((5, 4))
    kernel_of(6, 2)
    share((5, 4))
    spread((6, 3))
    if zs:
        for copy in tg_sent:
            copy.wait_recv()
    tt[...] = tg[...].T
    spread((5, 4))

    total = predv[quart_at(j), lane_of(0)]
    for s in (0, 1, 7, 2, 6, 3, 5, 4):
        for k in (0, 1):
            if (s, k) in quart_sent:
                quart_sent[s, k].wait_recv()
                total = total + qrecv[PLACE[(RING - s) % RING], k].astype(F32)
    mine_now = total - tt[quart_at(j), :]
    res[0, quart_at(j), :] = mine_now.astype(BF16)
    rq[quart_at(j), :] = mine_now
    if zs:
        quarter = res.at[0, quart_at(j)]
        res_x = send(quarter, quarter, facing)
        res_z = {}

        def res_send(way, dist, stream, hops):
            rows_of = quart_at((j, jx)[stream])
            here = PLACE[(-way * (dist - hops)) % RING]
            there = PLACE[(-way * dist) % RING]
            res_z[way, dist, stream] = send(
                res.at[here, rows_of], res.at[there, rows_of], at(z + way * hops, x, c)
            )

        for dist in (2, 1):
            for way in (1, -1):
                res_send(way, dist, 0, dist)
        res_x.wait_recv()
        for dist in (2, 1):
            for way in (1, -1):
                res_send(way, dist, 1, dist)
        res_mate = {}

        def res_pass(slot):
            block = res.at[PLACE[slot], half_at(c)]
            res_mate[slot] = send(block, block, partner)

        res_pass(0)
        wide_q = rq.at[quart_at(j)]
        rq_sent = [send(wide_q, wide_q, dev) for dev in (partner, facing, across)]
        for stream in (0, 1):
            for way in (1, -1):
                res_z[way, 2, stream].wait_recv()
                if (way == 1) == (stream == 0):
                    res_send(way, 4, stream, 2)
                res_send(way, 3, stream, 1)
        for dist in (1, 2, 3):
            for way in (1, -1):
                if dist != 2:
                    res_z[way, dist, 0].wait_recv()
                    res_z[way, dist, 1].wait_recv()
                res_pass((-way * dist) % RING)
        res_z[1, 4, 0].wait_recv()
        res_z[-1, 4, 1].wait_recv()
        res_pass(4)

    def res_ready(slots):
        if zs:
            for s in slots:
                res_mate[s].wait_recv()

    def gradient(p0, n, first):
        cols = slice(p0 * lanes, (p0 + n) * lanes)
        left = jnp.concatenate([res[p, 0:og, :] for p in range(p0, p0 + n)], axis=1)

        def part(n0, width):
            n0 = pl.multiple_of(n0, 128)
            term = dot(left, kt[pl.ds(n0, width), cols], NT)
            if first:
                gp[:, pl.ds(n0, width)] = term
            else:
                gpb[:, pl.ds(n0, width)] = (gp[:, pl.ds(n0, width)] + term).astype(BF16)

        over(pm // 256, lambda n0: part(n0, 256))
        part(pm, pp - pm)

    res_ready((0, 1, 7, 2, 6, 3))
    gradient(0, 6, True)
    res_ready((5, 4))
    gradient(6, 2, False)

    def own_term(s):
        col = lax.rem(y + s + RING, RING) * chunk
        return dot(gpb[...], oht[:, pl.ds(pl.multiple_of(col, 128), chunk)], NN)

    rows_p, rows_q = slice(0, top), slice(top, og)
    first_p = {1: slice(0, mid_p), -1: slice(mid_p, top)}
    first_q = {1: slice(top, mid_q), -1: slice(mid_q, og)}
    if ys:
        beside = at_y(y, 1 - xl)
        chain = {}
        swap = {}

        def term(s):
            whole = own_term(s)
            for h in (0, 1):
                terms[s % RING, h] = whole[:, h * sub : (h + 1) * sub]
            xps[s % RING] = terms[s % RING, 1 - xl, rows_p, :].astype(BF16)
            swap[s % RING] = send(xps.at[s % RING], xpr.at[s % RING], beside)

        def pass_on(kind, t, own, part, first, buffer, landed, h):
            for w, way in enumerate((1, -1)):
                s = (way * (5 - t)) % RING
                mine = own(s)
                base = part.start
                near_rows = slice(first[way].start - base, first[way].stop - base)
                out_at, in_at = buffer.at[w, t - 1, h], landed.at[w, t - 1, h]
                if t == 1:
                    out_at, in_at = out_at.at[near_rows], in_at.at[near_rows]
                    buffer[w, 0, h, near_rows, :] = mine[near_rows].astype(BF16)
                else:
                    chain[kind, way, t - 1, h].wait_recv()
                    if t == 2:
                        other = first[-way]
                        far_rows = slice(other.start - base, other.stop - base)
                        buffer[w, 1, h, near_rows, :] = (
                            mine[near_rows] + landed[w, 0, h, near_rows, :].astype(F32)
                        ).astype(BF16)
                        buffer[w, 1, h, far_rows, :] = mine[far_rows].astype(BF16)
                    else:
                        buffer[w, t - 1, h] = (
                            mine + landed[w, t - 2, h].astype(F32)
                        ).astype(BF16)
                chain[kind, way, t, h] = send(out_at, in_at, at_y(y + way, xl))

        def pass_q(t):
            for h in (0, 1):
                pass_on(
                    "q", t, lambda s, h=h: terms[s, h, rows_q, :], rows_q, first_q, yqs, yqr, h
                )

        def both_x(s):
            if s in swap:
                swap.pop(s).wait_recv()
                terms[s, xl, rows_p, :] += xpr[s].astype(F32)
            return terms[s, xl, rows_p, :]

        def pass_p(t):
            pass_on("p", t, both_x, rows_p, first_p, yps, ypr, 0)

        term(4)
        pass_q(1)
        term(3)
        term(5)
        pass_q(2)
        pass_p(1)
        term(2)
        term(6)
        pass_q(3)
        pass_p(2)
        term(1)
        term(7)
        pass_q(4)
        term(0)
        pass_p(3)
        for h in (0, 1):
            chain["q", 1, 4, h].wait_recv()
            chain["q", -1, 4, h].wait_recv()
            terms[0, h, rows_q, :] += yqr[0, 3, h].astype(F32) + yqr[1, 3, h].astype(F32)
        xsend[...] = terms[0, 1 - xl, rows_q, :].astype(BF16)
        swap_q = send(xsend, xrecv, beside)
        pass_p(4)
        sum_p = both_x(0)
        chain["p", 1, 4, 0].wait_recv()
        chain["p", -1, 4, 0].wait_recv()
        sum_p = sum_p + ypr[0, 3, 0].astype(F32) + ypr[1, 3, 0].astype(F32)
        grad[0, xl, rows_p, :] = sum_p.astype(BF16)
        swap_q.wait_recv()
        grad[0, xl, rows_q, :] = (terms[0, xl, rows_q, :] + xrecv[...].astype(F32)).astype(BF16)
        own = grad.at[0, xl]
        back = {}
        for way, slot in ((1, RING - 1), (-1, 1)):
            back[way, 1, 0] = send(own, grad.at[slot, xl], at_y(y + way, xl))
        cross_l = send(own, own, beside)
    else:
        for s in range(RING):
            for h in (0, 1):
                grad[s, h] = own_term(s)[:, h * sub : (h + 1) * sub].astype(BF16)

    stores = []

    def store(s, h):
        col = lax.rem(y + s, RING) * chunk + h * sub
        copy = pltpu.make_async_copy(
            grad.at[s, h],
            grad_out.at[:, pl.ds(pl.multiple_of(col, 128), sub)],
            osem.at[len(stores)],
        )
        copy.start()
        stores.append(copy)

    if ys:
        store(0, xl)
        cross_l.wait_recv()
        for way, slot in ((1, RING - 1), (-1, 1)):
            back[way, 1, 1] = send(
                grad.at[0, 1 - xl, rows_q], grad.at[slot, 1 - xl, rows_q], at_y(y + way, xl)
            )
        store(0, 1 - xl)
        beside_sent = {}
        last_way = {1: slice(0, split), -1: slice(split, og)}

        def give(slot):
            block = grad.at[slot, xl, rows_p]
            beside_sent[slot] = send(block, block, beside)
            store(slot, xl)

        for level in range(1, 4):
            for way in (1, -1):
                slot = slot_of(way, level)
                nxt = slot_of(way, level + 1)
                back[way, level, 0].wait_recv()
                part = last_way[way] if level == 3 else slice(0, og)
                back[way, level + 1, 0] = send(
                    grad.at[slot, xl, part], grad.at[nxt, xl, part], at_y(y + way, xl)
                )
                give(slot)
            for way in (1, -1):
                slot = slot_of(way, level)
                nxt = slot_of(way, level + 1)
                back[way, level, 1].wait_recv()
                if level < 3 or way == -1:
                    back[way, level + 1, 1] = send(
                        grad.at[slot, 1 - xl, rows_q], grad.at[nxt, 1 - xl, rows_q],
                        at_y(y + way, xl),
                    )
            if level == 1 and zs:
                for copy in rq_sent:
                    copy.wait_recv()
                rt[...] = rq[...].T
                res_out[...] = rt[rows_at(j), 0:out]
            if level > 1:
                for way in (1, -1):
                    slot = slot_of(way, level - 1)
                    beside_sent[slot].wait_recv()
                    store(slot, 1 - xl)
        back[1, 4, 0].wait_recv()
        back[-1, 4, 0].wait_recv()
        give(4)
        back[-1, 4, 1].wait_recv()
        for slot in (5, 3, 4):
            beside_sent[slot].wait_recv()
            store(slot, 1 - xl)
    else:
        for s in range(RING):
            for h in (0, 1):
                store(s, h)
        if zs:
            for copy in rq_sent:
                copy.wait_recv()
        rt[...] = rq[...].T
        res_out[...] = rt[rows_at(j), 0:out]
    for copy in stores:
        copy.wait()
    for copy in started:
        copy.wait_send()


def on_device(zs, ys, bpool, bidx, cpool, cidx, tgt, coef):
    rows, d = bidx.shape[0], bpool.shape[1]
    out, cen = tgt.shape[1], cidx.shape[0]
    n_pool = cpool.shape[0]
    outp, og = up(out, 64), up(out, 16)
    pp = n_pool // 256 * 256 + 128
    lanes = 4 * rows
    half, quart = outp // 2, outp // 4
    wide = up(outp, 128)
    chunk = cen // RING
    sub = chunk // 2
    top = up(og * 9 // 16, 16)
    vmem = pl.BlockSpec(memory_space=pltpu.VMEM)
    hbm = pl.BlockSpec(memory_space=pl.ANY)
    tail = pl.BlockSpec((16, d), lambda i: (n_pool // 256 * 16, 0))
    grad, residual = pl.pallas_call(
        functools.partial(step_kernel, zs, ys),
        out_shape=(
            jax.ShapeDtypeStruct((og, cen), BF16),
            jax.ShapeDtypeStruct((rows, out), F32),
        ),
        grid=(1,),
        in_specs=[vmem, vmem, vmem, hbm, tail, vmem, hbm],
        out_specs=(hbm, vmem),
        scratch_shapes=[
            pltpu.VMEM((up(bpool.shape[0], 16), d), BF16),
            pltpu.VMEM((RING, lanes, d), BF16),
            pltpu.VMEM((up(n_pool, 16), d), BF16),
            pltpu.VMEM((pp, 128), F32),
            pltpu.VMEM((pp, cen), BF16),
            pltpu.VMEM((out, cen), F32),
            pltpu.VMEM((og, cen), BF16),
            pltpu.VMEM((outp, pp), BF16),
            pltpu.VMEM((pp, RING * lanes), BF16),
            pltpu.VMEM((outp, RING * lanes), F32),
            pltpu.VMEM((RING, half, lanes), BF16),
            pltpu.VMEM((RING, half, lanes), BF16),
            pltpu.VMEM((RING, 2, quart, lanes), BF16),
            pltpu.VMEM((RING, 2, quart, lanes), BF16),
            pltpu.VMEM((lanes, wide), F32),
            pltpu.VMEM((wide, lanes), F32),
            pltpu.VMEM((RING, outp, lanes), BF16),
            pltpu.VMEM((outp, lanes), F32),
            pltpu.VMEM((lanes, outp), F32),
            pltpu.VMEM((og, pp), F32),
            pltpu.VMEM((og, pp), BF16),
            pltpu.VMEM((RING, 2, og, sub), F32),
            pltpu.VMEM((RING, top, sub), BF16),
            pltpu.VMEM((RING, top, sub), BF16),
            pltpu.VMEM((2, 4, 1, top, sub), BF16),
            pltpu.VMEM((2, 4, 1, top, sub), BF16),
            pltpu.VMEM((2, 4, 2, og - top, sub), BF16),
            pltpu.VMEM((2, 4, 2, og - top, sub), BF16),
            pltpu.VMEM((og - top, sub), BF16),
            pltpu.VMEM((og - top, sub), BF16),
            pltpu.VMEM((RING, 2, og, sub), BF16),
            pltpu.SemaphoreType.DMA((COPIES,)),
            pltpu.SemaphoreType.DMA((COPIES,)),
            pltpu.SemaphoreType.DMA((2,)),
            pltpu.SemaphoreType.DMA((2 * RING,)),
        ],
        compiler_params=pltpu.CompilerParams(
            collective_id=0, has_side_effects=True, vmem_limit_bytes=48 * 1024 * 1024
        ),
        name="regression_step",
    )(
        bidx.reshape(1, rows), bpool, cidx.reshape(1, cen), cpool, cpool, tgt, coef.T,
    )
    batch_total = rows * lax.axis_size("batch") * lax.axis_size("centre")
    step_size = 8.0 / math.sqrt(batch_total)
    updated = coef - step_size * grad[:out].astype(F32).T
    return updated, residual


def solution(mesh):
    both = ("batch", "centre")
    zs, ys = mesh.shape["centre"] > 1, mesh.shape["batch"] > 1
    return jax.shard_map(
        functools.partial(on_device, zs, ys),
        mesh=mesh,
        in_specs=(
            P(both, None), P(both), P("centre", None), P("centre"), P(both, None), P("centre", None),
        ),
        out_specs=(P("centre", None), P(both, None)),
        check_vma=False,
    )
```

```python
import functools
import math

import jax
import jax.numpy as jnp
from jax import lax
from jax.experimental import pallas as pl
from jax.experimental.pallas import tpu as pltpu
from jax.sharding import PartitionSpec as P

MESH = pl.DeviceIdType.MESH
F32 = jnp.float32
BF16 = jnp.bfloat16
RING = 8
NT = (((1,), (1,)), ((), ()))
NN = (((1,), (0,)), ((), ()))
TN = (((0,), (0,)), ((), ()))
PLACE = (0, 1, 3, 5, 7, 6, 4, 2)
COPIES = 176
LOG2E = 1.4426950408889634


def up(n, k):
    return -(-n // k) * k


def dot(a, b, dims):
    return lax.dot_general(a, b, dims, preferred_element_type=F32)


def step_kernel(*refs):
    inner_kernel([], *refs)


def inner_kernel(
    started, zs, ys, bidx, bpool, cidx, cpool, ctail, tgt, coef, grad_out, res_out,
    bsel, xall, pool, cs, oht, coefv, coefb, coefp, kt, predv, psend, precv,
    qsend, qrecv, tg, tt, res, rq, rt, gp, gpb, terms, xps, xpr, yps, ypr, yqs, yqr, xsend, xrecv, grad,
    ssem, rsem, lsem, osem,
):
    bi = lax.axis_index("batch")
    ci = lax.axis_index("centre")
    y, xl = bi // 2, bi % 2
    z, x, c = ci // 4, (ci // 2) % 2, ci % 2
    rows, d = tgt.shape[0], bpool.shape[1]
    out = tgt.shape[1]
    cen = cidx.shape[1]
    n_pool = cpool.shape[0]
    pp = kt.shape[0]
    pm = n_pool // 256 * 256
    full = pool.shape[0]
    tall = full // 5 if full % 80 == 0 else 16
    lanes = 4 * rows
    half, quart = predv.shape[0] // 2, predv.shape[0] // 4
    og = gp.shape[0]
    top = xps.shape[1]
    mid_p = up(top // 2, 16)
    mid_q = top + up((og - top) // 2, 16)
    chunk = cen // RING
    sub = chunk // 2

    def at(z_, x_, c_):
        return (bi, lax.rem(z_ + 2 * RING, RING) * 4 + x_ * 2 + c_)

    def at_y(y_, xl_):
        return (lax.rem(y_ + 2 * RING, RING) * 2 + xl_, ci)

    count = [0]
    def send(src, dst, dev):
        n = count[0]
        count[0] += 1
        copy = pltpu.make_async_remote_copy(
            src_ref=src, dst_ref=dst, send_sem=ssem.at[n], recv_sem=rsem.at[n],
            device_id=dev, device_id_type=MESH,
        )
        copy.start()
        started.append(copy)
        return copy

    partner = at(z, x, 1 - c)
    facing = at(z, 1 - x, c)
    across = at(z, 1 - x, 1 - c)
    greet = []
    if zs:
        greet += [partner, facing, across]
        greet += [at(z + s, x, c) for s in range(1, RING)]
        greet += [at(z + s, 1 - x, c) for s in range(1, RING)]
    if ys:
        greet += [at_y(y + 1, xl), at_y(y - 1, xl), at_y(y, 1 - xl)]
    barrier = pltpu.get_barrier_semaphore()
    for dev in greet:
        pl.semaphore_signal(barrier, inc=1, device_id=dev, device_id_type=MESH)

    load_pool = pltpu.make_async_copy(cpool.at[0:pm], pool.at[0:pm], lsem.at[0])
    load_pool.start()
    load_coef = pltpu.make_async_copy(coef, coefv, lsem.at[1])
    load_coef.start()

    def over(n, body):
        times = 3 if n % 3 == 0 else 1

        def group(m, carry):
            for k in range(times):
                body((m * times + k) * 256)
            return carry

        lax.fori_loop(0, n // times, group, 0)

    def rows_at(k):
        return pl.ds(pl.multiple_of(k * rows, rows), rows)

    def quart_at(k):
        return pl.ds(pl.multiple_of(k * quart, 16), quart)

    def half_at(k):
        return pl.ds(pl.multiple_of(k * half, 16), half)

    j = c * 2 + x
    jx = c * 2 + 1 - x

    bsel[...] = jnp.zeros_like(bsel)
    bsel[0 : bpool.shape[0], :] = bpool[...]
    base = (bi * lax.axis_size("centre") + ci) * bpool.shape[0]
    place = lax.broadcasted_iota(jnp.int32, (bsel.shape[0], rows), 0) + base
    pick = jnp.where(place == bidx[...], -2.0, 0.0).astype(BF16)
    xall[0, rows_at(j), :] = dot(pick, bsel[...], TN).astype(BF16)
    tg[rows_at(j), :] = jnp.zeros((rows, tg.shape[1]), F32)
    tg[rows_at(j), 0:out] = tgt[...]

    cbase = ci * n_pool
    step_rows = 32

    def build(m, carry):
        r0 = pl.multiple_of(m * step_rows, step_rows)
        at_row = lax.broadcasted_iota(jnp.int32, (step_rows, cen), 0) + (cbase + r0)
        oht[pl.ds(r0, step_rows), :] = jnp.where(at_row == cidx[...], 1.0, 0.0).astype(BF16)
        return carry

    lax.fori_loop(0, pp // step_rows, build, 0)

    pl.semaphore_wait(barrier, len(greet))

    ring = {}
    mate = {}
    if zs:
        own = xall.at[0, rows_at(j)]
        cross_x = send(own, own, facing)
        for way, slot in ((1, RING - 1), (-1, 1)):
            ring[way, 1, 0] = send(own, xall.at[PLACE[slot], rows_at(j)], at(z + way, x, c))
        mate[0, 0] = send(own, own, partner)

    def slot_of(way, level):
        return RING - level if way == 1 else level

    def forward(level):
        if not zs:
            return
        for stream, place_of in ((0, j), (1, jx)):
            for way in (1, -1):
                if level == 0:
                    if way == 1:
                        if stream == 0:
                            continue
                        cross_x.wait_recv()
                        block = xall.at[0, rows_at(jx)]
                        mate[0, 1] = send(block, block, partner)
                    elif stream == 0:
                        continue
                else:
                    if level == 4 and (way == 1) != (stream == 0):
                        continue
                    ring[way, level, stream].wait_recv()
                slot = slot_of(way, level) % RING
                block = xall.at[PLACE[slot], rows_at(place_of)]
                if level < 4 and (level < 3 or (way == 1) == (stream == 0)):
                    nxt = slot_of(way, level + 1)
                    ring[way, level + 1, stream] = send(
                        block, xall.at[PLACE[nxt], rows_at(place_of)], at(z + way, x, c)
                    )
                if level:
                    mate[slot, stream] = send(block, block, partner)

    def ready(slots):
        if zs:
            for s in slots:
                mate[s, 0].wait_recv()
                mate[s, 1].wait_recv()

    load_pool.wait()
    last = ctail[...]
    real = lax.broadcasted_iota(jnp.int32, last.shape, 0) < n_pool - pm
    pool[pm:full, :] = jnp.where(real, last, jnp.zeros_like(last))

    def squares(r0, n):
        wide = pool[pl.ds(r0, n), :].astype(F32)
        cs[pl.ds(r0, n), :] = jnp.broadcast_to(
            jnp.sum(wide * wide, axis=1, keepdims=True), (n, 128)
        )

    over(pm // 256, lambda r0: squares(pl.multiple_of(r0, 256), 256))
    squares(pm, full - pm)
    kt[full:, :] = jnp.zeros_like(kt[full:, :])
    forward(0)

    load_coef.wait()
    coefb[...] = jnp.zeros_like(coefb)
    coefb[0:out, :] = coefv[...].astype(BF16)
    if og < coefp.shape[0]:
        coefp[og:, :] = jnp.zeros_like(coefp[og:, :])

    def permute(n, width):
        n = pl.multiple_of(n, 128)
        coefp[0:og, pl.ds(n, width)] = dot(
            coefb[...], oht[pl.ds(n, width), :], NT
        ).astype(BF16)

    def near(squared):
        floor = jnp.maximum(squared, 1e-30)
        return jnp.exp2(floor * lax.rsqrt(floor) * -LOG2E).astype(BF16)

    def kernel_of(p0, n, level=None):
        width = n * lanes
        cols = slice(p0 * lanes, p0 * lanes + width)
        feats = xall[p0 : p0 + n].reshape(width, d)
        wide = feats.astype(F32)
        size = jnp.sum(wide * wide, axis=1, keepdims=True) * 0.25
        row = jnp.broadcast_to(size, (width, 128)).T[0:1, :]

        for r0 in range(0, full, tall):
            r1 = r0 + tall
            both = dot(pool[r0:r1, :], xall[p0 : p0 + n].reshape(width, d), NT)
            col = cs[r0:r1, :]
            col = jnp.concatenate([col] * (width // 128), axis=1) if width > 128 else col[:, :width]
            kt[r0:r1, cols] = near(row + col + both)
            if r0 == tall and level is not None:
                forward(level)
        predv[:, cols] = dot(coefp[...], kt[:, cols], NN)

    core_sent = {}
    quart_sent = {}

    def lane_of(s):
        return slice(PLACE[s] * lanes, (PLACE[s] + 1) * lanes)

    def share(slots):
        if zs:
            for s in slots:
                psend[PLACE[s]] = predv[half_at(1 - c), lane_of(s)].astype(BF16)
                core_sent[s] = send(psend.at[PLACE[s]], precv.at[PLACE[s]], partner)

    def spread(slots):
        if not zs:
            return
        for s in slots:
            core_sent[s].wait_recv()
            predv[half_at(c), lane_of(s)] += precv[PLACE[s]].astype(F32)
            back = PLACE[(RING - s) % RING]
            for k, xd in ((0, x), (1, 1 - x)):
                if s == 0 and k == 0:
                    continue
                qsend[PLACE[s], k] = predv[quart_at(c * 2 + xd), lane_of(s)].astype(BF16)
                quart_sent[s, k] = send(
                    qsend.at[PLACE[s], k], qrecv.at[back, k], at(z + s, xd, c)
                )

    cuts = (0, pm // 768 * 512, pm) if pm % 768 == 0 else (0, 0, pm)
    over((cuts[1] - cuts[0]) // 256, lambda n0: permute(n0, 256))
    forward(1)
    over((cuts[2] - cuts[1]) // 256, lambda n0: permute(cuts[1] + n0, 256))
    permute(pm, pp - pm)
    if zs:
        mine = tg.at[rows_at(j)]
        tg_sent = [send(mine, mine, dev) for dev in (partner, facing, across)]
    ready((0, 1))
    kernel_of(0, 2, 2)
    share((0, 1))
    ready((7, 2))
    kernel_of(2, 2, 3)
    share((7, 2))
    spread((0, 1))
    ready((6, 3))
    kernel_of(4, 2)
    share((6, 3))
    spread((7, 2))
    forward(4)
    ready((5, 4))
    kernel_of(6, 2)
    share((5, 4))
    spread((6, 3))
    if zs:
        for copy in tg_sent:
            copy.wait_recv()
    tt[...] = tg[...].T
    spread((5, 4))

    total = predv[quart_at(j), lane_of(0)]
    for s in (0, 1, 7, 2, 6, 3, 5, 4):
        for k in (0, 1):
            if (s, k) in quart_sent:
                quart_sent[s, k].wait_recv()
                total = total + qrecv[PLACE[(RING - s) % RING], k].astype(F32)
    mine_now = total - tt[quart_at(j), :]
    res[0, quart_at(j), :] = mine_now.astype(BF16)
    rq[quart_at(j), :] = mine_now
    if zs:
        quarter = res.at[0, quart_at(j)]
        res_x = send(quarter, quarter, facing)
        res_z = {}

        def res_send(way, dist, stream, hops):
            rows_of = quart_at((j, jx)[stream])
            here = PLACE[(-way * (dist - hops)) % RING]
            there = PLACE[(-way * dist) % RING]
            res_z[way, dist, stream] = send(
                res.at[here, rows_of], res.at[there, rows_of], at(z + way * hops, x, c)
            )

        for dist in (2, 1):
            for way in (1, -1):
                res_send(way, dist, 0, dist)
        res_x.wait_recv()
        for dist in (2, 1):
            for way in (1, -1):
                res_send(way, dist, 1, dist)
        res_mate = {}

        def res_pass(slot):
            block = res.at[PLACE[slot], half_at(c)]
            res_mate[slot] = send(block, block, partner)

        res_pass(0)
        wide_q = rq.at[quart_at(j)]
        rq_sent = [send(wide_q, wide_q, dev) for dev in (partner, facing, across)]
        for stream in (0, 1):
            for way in (1, -1):
                res_z[way, 2, stream].wait_recv()
                if (way == 1) == (stream == 0):
                    res_send(way, 4, stream, 2)
                res_send(way, 3, stream, 1)
        for dist in (1, 2, 3):
            for way in (1, -1):
                if dist != 2:
                    res_z[way, dist, 0].wait_recv()
                    res_z[way, dist, 1].wait_recv()
                res_pass((-way * dist) % RING)
        res_z[1, 4, 0].wait_recv()
        res_z[-1, 4, 1].wait_recv()
        res_pass(4)

    def res_ready(slots):
        if zs:
            for s in slots:
                res_mate[s].wait_recv()

    def gradient(p0, n, first):
        cols = slice(p0 * lanes, (p0 + n) * lanes)
        left = jnp.concatenate([res[p, 0:og, :] for p in range(p0, p0 + n)], axis=1)

        def part(n0, width):
            n0 = pl.multiple_of(n0, 128)
            term = dot(left, kt[pl.ds(n0, width), cols], NT)
            if first:
                gp[:, pl.ds(n0, width)] = term
            else:
                gpb[:, pl.ds(n0, width)] = (gp[:, pl.ds(n0, width)] + term).astype(BF16)

        over(pm // 256, lambda n0: part(n0, 256))
        part(pm, pp - pm)

    res_ready((0, 1, 7, 2, 6, 3))
    gradient(0, 6, True)
    res_ready((5, 4))
    gradient(6, 2, False)

    def own_term(s):
        col = lax.rem(y + s + RING, RING) * chunk
        return dot(gpb[...], oht[:, pl.ds(pl.multiple_of(col, 128), chunk)], NN)

    rows_p, rows_q = slice(0, top), slice(top, og)
    first_p = {1: slice(0, mid_p), -1: slice(mid_p, top)}
    first_q = {1: slice(top, mid_q), -1: slice(mid_q, og)}
    if ys:
        beside = at_y(y, 1 - xl)
        chain = {}
        swap = {}

        def term(s):
            whole = own_term(s)
            for h in (0, 1):
                terms[s % RING, h] = whole[:, h * sub : (h + 1) * sub]
            xps[s % RING] = terms[s % RING, 1 - xl, rows_p, :].astype(BF16)
            swap[s % RING] = send(xps.at[s % RING], xpr.at[s % RING], beside)

        def pass_on(kind, t, own, part, first, buffer, landed, h):
            for w, way in enumerate((1, -1)):
                s = (way * (5 - t)) % RING
                mine = own(s)
                base = part.start
                near_rows = slice(first[way].start - base, first[way].stop - base)
                out_at, in_at = buffer.at[w, t - 1, h], landed.at[w, t - 1, h]
                if t == 1:
                    out_at, in_at = out_at.at[near_rows], in_at.at[near_rows]
                    buffer[w, 0, h, near_rows, :] = mine[near_rows].astype(BF16)
                else:
                    chain[kind, way, t - 1, h].wait_recv()
                    if t == 2:
                        other = first[-way]
                        far_rows = slice(other.start - base, other.stop - base)
                        buffer[w, 1, h, near_rows, :] = (
                            mine[near_rows] + landed[w, 0, h, near_rows, :].astype(F32)
                        ).astype(BF16)
                        buffer[w, 1, h, far_rows, :] = mine[far_rows].astype(BF16)
                    else:
                        buffer[w, t - 1, h] = (
                            mine + landed[w, t - 2, h].astype(F32)
                        ).astype(BF16)
                chain[kind, way, t, h] = send(out_at, in_at, at_y(y + way, xl))

        def pass_q(t):
            for h in (0, 1):
                pass_on(
                    "q", t, lambda s, h=h: terms[s, h, rows_q, :], rows_q, first_q, yqs, yqr, h
                )

        def both_x(s):
            if s in swap:
                swap.pop(s).wait_recv()
                terms[s, xl, rows_p, :] += xpr[s].astype(F32)
            return terms[s, xl, rows_p, :]

        def pass_p(t):
            pass_on("p", t, both_x, rows_p, first_p, yps, ypr, 0)

        term(4)
        pass_q(1)
        term(3)
        term(5)
        pass_q(2)
        pass_p(1)
        term(2)
        term(6)
        pass_q(3)
        pass_p(2)
        term(1)
        term(7)
        pass_q(4)
        term(0)
        pass_p(3)
        for h in (0, 1):
            chain["q", 1, 4, h].wait_recv()
            chain["q", -1, 4, h].wait_recv()
            terms[0, h, rows_q, :] += yqr[0, 3, h].astype(F32) + yqr[1, 3, h].astype(F32)
        xsend[...] = terms[0, 1 - xl, rows_q, :].astype(BF16)
        swap_q = send(xsend, xrecv, beside)
        pass_p(4)
        sum_p = both_x(0)
        chain["p", 1, 4, 0].wait_recv()
        chain["p", -1, 4, 0].wait_recv()
        sum_p = sum_p + ypr[0, 3, 0].astype(F32) + ypr[1, 3, 0].astype(F32)
        grad[0, xl, rows_p, :] = sum_p.astype(BF16)
        back = {}

        def copy_back(part, way, level):
            h = 1 - xl if part == "b" else xl
            rows_of = rows_p if part == "p" else rows_q
            here = slot_of(way, level - 1) % RING
            back[part, way, level] = send(
                grad.at[here, h, rows_of], grad.at[slot_of(way, level), h, rows_of],
                at_y(y + way, xl),
            )

        def give(slot, rows_of=rows_p):
            block = grad.at[slot, xl, rows_of]
            return send(block, block, beside)

        copy_back("p", 1, 1)
        copy_back("p", -1, 1)
        beside_sent = {0: give(0)}
        swap_q.wait_recv()
        grad[0, xl, rows_q, :] = (terms[0, xl, rows_q, :] + xrecv[...].astype(F32)).astype(BF16)
        beside_q = give(0, rows_q)
        copy_back("q", 1, 1)
        copy_back("q", -1, 1)
    else:
        for s in range(RING):
            for h in (0, 1):
                grad[s, h] = own_term(s)[:, h * sub : (h + 1) * sub].astype(BF16)

    stores = []

    def store(s, h):
        col = lax.rem(y + s, RING) * chunk + h * sub
        copy = pltpu.make_async_copy(
            grad.at[s, h],
            grad_out.at[:, pl.ds(pl.multiple_of(col, 128), sub)],
            osem.at[len(stores)],
        )
        copy.start()
        stores.append(copy)

    if ys:
        store(0, xl)
        beside_q.wait_recv()
        copy_back("b", 1, 1)
        copy_back("b", -1, 1)
        beside_sent[0].wait_recv()
        store(0, 1 - xl)
        for level in range(1, 5):
            for part in ("p", "q", "b"):
                only = 1 if part == "p" else -1
                for way in (1, -1) if level < 4 else (only,):
                    slot = slot_of(way, level)
                    back[part, way, level].wait_recv()
                    if level < 3 or (level == 3 and way == only):
                        copy_back(part, way, level + 1)
                    if part == "p":
                        beside_sent[slot] = give(slot)
                    elif part == "q":
                        store(slot, xl)
            if level == 1 and zs:
                for copy in rq_sent:
                    copy.wait_recv()
                rt[...] = rq[...].T
                res_out[...] = rt[rows_at(j), 0:out]
        for slot in (7, 1, 6, 2, 5, 3, 4):
            beside_sent[slot].wait_recv()
            store(slot, 1 - xl)
    else:
        for s in range(RING):
            for h in (0, 1):
                store(s, h)
        if zs:
            for copy in rq_sent:
                copy.wait_recv()
        rt[...] = rq[...].T
        res_out[...] = rt[rows_at(j), 0:out]
    for copy in stores:
        copy.wait()
    for copy in started:
        copy.wait_send()


def on_device(zs, ys, bpool, bidx, cpool, cidx, tgt, coef):
    rows, d = bidx.shape[0], bpool.shape[1]
    out, cen = tgt.shape[1], cidx.shape[0]
    n_pool = cpool.shape[0]
    outp, og = up(out, 64), up(out, 16)
    pp = n_pool // 256 * 256 + 128
    lanes = 4 * rows
    half, quart = outp // 2, outp // 4
    wide = up(outp, 128)
    chunk = cen // RING
    sub = chunk // 2
    top = up(og * 9 // 16, 16)
    vmem = pl.BlockSpec(memory_space=pltpu.VMEM)
    hbm = pl.BlockSpec(memory_space=pl.ANY)
    tail = pl.BlockSpec((16, d), lambda i: (n_pool // 256 * 16, 0))
    grad, residual = pl.pallas_call(
        functools.partial(step_kernel, zs, ys),
        out_shape=(
            jax.ShapeDtypeStruct((og, cen), BF16),
            jax.ShapeDtypeStruct((rows, out), F32),
        ),
        grid=(1,),
        in_specs=[vmem, vmem, vmem, hbm, tail, vmem, hbm],
        out_specs=(hbm, vmem),
        scratch_shapes=[
            pltpu.VMEM((up(bpool.shape[0], 16), d), BF16),
            pltpu.VMEM((RING, lanes, d), BF16),
            pltpu.VMEM((up(n_pool, 16), d), BF16),
            pltpu.VMEM((pp, 128), F32),
            pltpu.VMEM((pp, cen), BF16),
            pltpu.VMEM((out, cen), F32),
            pltpu.VMEM((og, cen), BF16),
            pltpu.VMEM((outp, pp), BF16),
            pltpu.VMEM((pp, RING * lanes), BF16),
            pltpu.VMEM((outp, RING * lanes), F32),
            pltpu.VMEM((RING, half, lanes), BF16),
            pltpu.VMEM((RING, half, lanes), BF16),
            pltpu.VMEM((RING, 2, quart, lanes), BF16),
            pltpu.VMEM((RING, 2, quart, lanes), BF16),
            pltpu.VMEM((lanes, wide), F32),
            pltpu.VMEM((wide, lanes), F32),
            pltpu.VMEM((RING, outp, lanes), BF16),
            pltpu.VMEM((outp, lanes), F32),
            pltpu.VMEM((lanes, outp), F32),
            pltpu.VMEM((og, pp), F32),
            pltpu.VMEM((og, pp), BF16),
            pltpu.VMEM((RING, 2, og, sub), F32),
            pltpu.VMEM((RING, top, sub), BF16),
            pltpu.VMEM((RING, top, sub), BF16),
            pltpu.VMEM((2, 4, 1, top, sub), BF16),
            pltpu.VMEM((2, 4, 1, top, sub), BF16),
            pltpu.VMEM((2, 4, 2, og - top, sub), BF16),
            pltpu.VMEM((2, 4, 2, og - top, sub), BF16),
            pltpu.VMEM((og - top, sub), BF16),
            pltpu.VMEM((og - top, sub), BF16),
            pltpu.VMEM((RING, 2, og, sub), BF16),
            pltpu.SemaphoreType.DMA((COPIES,)),
            pltpu.SemaphoreType.DMA((COPIES,)),
            pltpu.SemaphoreType.DMA((2,)),
            pltpu.SemaphoreType.DMA((2 * RING,)),
        ],
        compiler_params=pltpu.CompilerParams(
            collective_id=0, has_side_effects=True, vmem_limit_bytes=48 * 1024 * 1024
        ),
        name="regression_step",
    )(
        bidx.reshape(1, rows), bpool, cidx.reshape(1, cen), cpool, cpool, tgt, coef.T,
    )
    batch_total = rows * lax.axis_size("batch") * lax.axis_size("centre")
    step_size = 8.0 / math.sqrt(batch_total)
    updated = coef - step_size * grad[:out].astype(F32).T
    return updated, residual


def solution(mesh):
    both = ("batch", "centre")
    zs, ys = mesh.shape["centre"] > 1, mesh.shape["batch"] > 1
    return jax.shard_map(
        functools.partial(on_device, zs, ys),
        mesh=mesh,
        in_specs=(
            P(both, None), P(both), P("centre", None), P("centre"), P(both, None), P("centre", None),
        ),
        out_specs=(P("centre", None), P(both, None)),
        check_vma=False,
    )
```

```python
import functools
import math

import jax
import jax.numpy as jnp
from jax import lax
from jax.experimental import pallas as pl
from jax.experimental.pallas import tpu as pltpu
from jax.sharding import PartitionSpec as P

MESH = pl.DeviceIdType.MESH
F32 = jnp.float32
BF16 = jnp.bfloat16
RING = 8
NT = (((1,), (1,)), ((), ()))
NN = (((1,), (0,)), ((), ()))
TN = (((0,), (0,)), ((), ()))
PLACE = (0, 1, 3, 5, 7, 6, 4, 2)
COPIES = 176
LOG2E = 1.4426950408889634


def up(n, k):
    return -(-n // k) * k


def dot(a, b, dims):
    return lax.dot_general(a, b, dims, preferred_element_type=F32)


def step_kernel(*refs):
    inner_kernel([], *refs)


def inner_kernel(
    started, zs, ys, bidx, bpool, cidx, cpool, ctail, tgt, coef, grad_out, res_out,
    bsel, xall, pool, cs, oht, coefv, coefb, coefp, kt, predv, psend, precv,
    qsend, qrecv, tg, tt, res, rq, rt, gp, gpb, terms, xps, xpr, yps, ypr, yqs, yqr, xsend, xrecv, grad,
    ssem, rsem, lsem, osem,
):
    bi = lax.axis_index("batch")
    ci = lax.axis_index("centre")
    y, xl = bi // 2, bi % 2
    z, x, c = ci // 4, (ci // 2) % 2, ci % 2
    rows, d = tgt.shape[0], bpool.shape[1]
    out = tgt.shape[1]
    cen = cidx.shape[1]
    n_pool = cpool.shape[0]
    pp = kt.shape[0]
    pm = n_pool // 256 * 256
    full = pool.shape[0]
    tall = full // 5 if full % 80 == 0 else 16
    lanes = 4 * rows
    half, quart = predv.shape[0] // 2, predv.shape[0] // 4
    og = gp.shape[0]
    top = xps.shape[1]
    mid_p = up(top // 2, 16)
    mid_q = top + up((og - top) // 2, 16)
    chunk = cen // RING
    sub = chunk // 2

    def at(z_, x_, c_):
        return (bi, lax.rem(z_ + 2 * RING, RING) * 4 + x_ * 2 + c_)

    def at_y(y_, xl_):
        return (lax.rem(y_ + 2 * RING, RING) * 2 + xl_, ci)

    count = [0]
    def send(src, dst, dev):
        n = count[0]
        count[0] += 1
        copy = pltpu.make_async_remote_copy(
            src_ref=src, dst_ref=dst, send_sem=ssem.at[n], recv_sem=rsem.at[n],
            device_id=dev, device_id_type=MESH,
        )
        copy.start()
        started.append(copy)
        return copy

    partner = at(z, x, 1 - c)
    facing = at(z, 1 - x, c)
    across = at(z, 1 - x, 1 - c)
    greet = []
    if zs:
        greet += [partner, facing, across]
        greet += [at(z + s, x, c) for s in range(1, RING)]
        greet += [at(z + s, 1 - x, c) for s in range(1, RING)]
    if ys:
        greet += [at_y(y + 1, xl), at_y(y - 1, xl), at_y(y, 1 - xl)]
    barrier = pltpu.get_barrier_semaphore()
    for dev in greet:
        pl.semaphore_signal(barrier, inc=1, device_id=dev, device_id_type=MESH)

    load_pool = pltpu.make_async_copy(cpool.at[0:pm], pool.at[0:pm], lsem.at[0])
    load_pool.start()
    load_coef = pltpu.make_async_copy(coef, coefv, lsem.at[1])
    load_coef.start()

    def over(n, body):
        times = 3 if n % 3 == 0 else 1

        def group(m, carry):
            for k in range(times):
                body((m * times + k) * 256)
            return carry

        lax.fori_loop(0, n // times, group, 0)

    def rows_at(k):
        return pl.ds(pl.multiple_of(k * rows, rows), rows)

    def quart_at(k):
        return pl.ds(pl.multiple_of(k * quart, 16), quart)

    def half_at(k):
        return pl.ds(pl.multiple_of(k * half, 16), half)

    j = c * 2 + x
    jx = c * 2 + 1 - x

    bsel[...] = jnp.zeros_like(bsel)
    bsel[0 : bpool.shape[0], :] = bpool[...]
    base = (bi * lax.axis_size("centre") + ci) * bpool.shape[0]
    place = lax.broadcasted_iota(jnp.int32, (bsel.shape[0], rows), 0) + base
    pick = jnp.where(place == bidx[...], -2.0, 0.0).astype(BF16)
    xall[0, rows_at(j), :] = dot(pick, bsel[...], TN).astype(BF16)
    tg[rows_at(j), :] = jnp.zeros((rows, tg.shape[1]), F32)
    tg[rows_at(j), 0:out] = tgt[...]

    cbase = ci * n_pool
    step_rows = 32

    def build(m, carry):
        r0 = pl.multiple_of(m * step_rows, step_rows)
        at_row = lax.broadcasted_iota(jnp.int32, (step_rows, cen), 0) + (cbase + r0)
        oht[pl.ds(r0, step_rows), :] = jnp.where(at_row == cidx[...], 1.0, 0.0).astype(BF16)
        return carry

    lax.fori_loop(0, pp // step_rows, build, 0)

    pl.semaphore_wait(barrier, len(greet))

    ring = {}
    mate = {}
    if zs:
        own = xall.at[0, rows_at(j)]
        cross_x = send(own, own, facing)
        for way, slot in ((1, RING - 1), (-1, 1)):
            ring[way, 1, 0] = send(own, xall.at[PLACE[slot], rows_at(j)], at(z + way, x, c))
        mate[0, 0] = send(own, own, partner)

    def slot_of(way, level):
        return RING - level if way == 1 else level

    def forward(level):
        if not zs:
            return
        for stream, place_of in ((0, j), (1, jx)):
            for way in (1, -1):
                if level == 0:
                    if way == 1:
                        if stream == 0:
                            continue
                        cross_x.wait_recv()
                        block = xall.at[0, rows_at(jx)]
                        mate[0, 1] = send(block, block, partner)
                    elif stream == 0:
                        continue
                else:
                    if level == 4 and (way == 1) != (stream == 0):
                        continue
                    ring[way, level, stream].wait_recv()
                slot = slot_of(way, level) % RING
                block = xall.at[PLACE[slot], rows_at(place_of)]
                if level < 4 and (level < 3 or (way == 1) == (stream == 0)):
                    nxt = slot_of(way, level + 1)
                    ring[way, level + 1, stream] = send(
                        block, xall.at[PLACE[nxt], rows_at(place_of)], at(z + way, x, c)
                    )
                if level:
                    mate[slot, stream] = send(block, block, partner)

    def ready(slots):
        if zs:
            for s in slots:
                mate[s, 0].wait_recv()
                mate[s, 1].wait_recv()

    load_pool.wait()
    last = ctail[...]
    real = lax.broadcasted_iota(jnp.int32, last.shape, 0) < n_pool - pm
    pool[pm:full, :] = jnp.where(real, last, jnp.zeros_like(last))

    def squares(r0, n):
        wide = pool[pl.ds(r0, n), :].astype(F32)
        cs[pl.ds(r0, n), :] = jnp.broadcast_to(
            jnp.sum(wide * wide, axis=1, keepdims=True), (n, 128)
        )

    over(pm // 256, lambda r0: squares(pl.multiple_of(r0, 256), 256))
    squares(pm, full - pm)
    kt[full:, :] = jnp.zeros_like(kt[full:, :])
    forward(0)

    load_coef.wait()
    coefb[...] = jnp.zeros_like(coefb)
    coefb[0:out, :] = coefv[...].astype(BF16)
    if og < coefp.shape[0]:
        coefp[og:, :] = jnp.zeros_like(coefp[og:, :])

    def permute(n, width):
        n = pl.multiple_of(n, 128)
        coefp[0:og, pl.ds(n, width)] = dot(
            coefb[...], oht[pl.ds(n, width), :], NT
        ).astype(BF16)

    def near(squared):
        floor = jnp.maximum(squared, 1e-30)
        return jnp.exp2(floor * lax.rsqrt(floor) * -LOG2E).astype(BF16)

    def kernel_of(p0, n, level=None):
        width = n * lanes
        cols = slice(p0 * lanes, p0 * lanes + width)
        feats = xall[p0 : p0 + n].reshape(width, d)
        wide = feats.astype(F32)
        size = jnp.sum(wide * wide, axis=1, keepdims=True) * 0.25
        row = jnp.broadcast_to(size, (width, 128)).T[0:1, :]

        for r0 in range(0, full, tall):
            r1 = r0 + tall
            both = dot(pool[r0:r1, :], xall[p0 : p0 + n].reshape(width, d), NT)
            col = cs[r0:r1, :]
            col = jnp.concatenate([col] * (width // 128), axis=1) if width > 128 else col[:, :width]
            kt[r0:r1, cols] = near(row + col + both)
            if r0 == tall and level is not None:
                forward(level)
        predv[:, cols] = dot(coefp[...], kt[:, cols], NN)

    core_sent = {}
    quart_sent = {}

    def lane_of(s):
        return slice(PLACE[s] * lanes, (PLACE[s] + 1) * lanes)

    def share(slots):
        if zs:
            for s in slots:
                psend[PLACE[s]] = predv[half_at(1 - c), lane_of(s)].astype(BF16)
                core_sent[s] = send(psend.at[PLACE[s]], precv.at[PLACE[s]], partner)

    def spread(slots):
        if not zs:
            return
        for s in slots:
            core_sent[s].wait_recv()
            predv[half_at(c), lane_of(s)] += precv[PLACE[s]].astype(F32)
            back = PLACE[(RING - s) % RING]
            for k, xd in ((0, x), (1, 1 - x)):
                if s == 0 and k == 0:
                    continue
                qsend[PLACE[s], k] = predv[quart_at(c * 2 + xd), lane_of(s)].astype(BF16)
                quart_sent[s, k] = send(
                    qsend.at[PLACE[s], k], qrecv.at[back, k], at(z + s, xd, c)
                )

    cuts = (0, pm // 768 * 512, pm) if pm % 768 == 0 else (0, 0, pm)
    over((cuts[1] - cuts[0]) // 256, lambda n0: permute(n0, 256))
    forward(1)
    over((cuts[2] - cuts[1]) // 256, lambda n0: permute(cuts[1] + n0, 256))
    permute(pm, pp - pm)
    if zs:
        mine = tg.at[rows_at(j)]
        tg_sent = [send(mine, mine, dev) for dev in (partner, facing, across)]
    ready((0, 1))
    kernel_of(0, 2, 2)
    share((0, 1))
    ready((7, 2))
    kernel_of(2, 2, 3)
    share((7, 2))
    spread((0, 1))
    ready((6, 3))
    kernel_of(4, 2)
    share((6, 3))
    spread((7, 2))
    forward(4)
    ready((5, 4))
    kernel_of(6, 2)
    share((5, 4))
    spread((6, 3))
    if zs:
        for copy in tg_sent:
            copy.wait_recv()
    tt[...] = tg[...].T
    spread((5, 4))

    total = predv[quart_at(j), lane_of(0)]
    for s in (0, 1, 7, 2, 6, 3, 5, 4):
        for k in (0, 1):
            if (s, k) in quart_sent:
                quart_sent[s, k].wait_recv()
                total = total + qrecv[PLACE[(RING - s) % RING], k].astype(F32)
    mine_now = total - tt[quart_at(j), :]
    res[0, quart_at(j), :] = mine_now.astype(BF16)
    rq[quart_at(j), :] = mine_now
    if zs:
        quarter = res.at[0, quart_at(j)]
        res_x = send(quarter, quarter, facing)
        res_z = {}

        def res_send(way, dist, stream, hops):
            rows_of = quart_at((j, jx)[stream])
            here = PLACE[(-way * (dist - hops)) % RING]
            there = PLACE[(-way * dist) % RING]
            res_z[way, dist, stream] = send(
                res.at[here, rows_of], res.at[there, rows_of], at(z + way * hops, x, c)
            )

        for dist in (2, 1):
            for way in (1, -1):
                res_send(way, dist, 0, dist)
        res_x.wait_recv()
        for dist in (2, 1):
            for way in (1, -1):
                res_send(way, dist, 1, dist)
        res_mate = {}

        def res_pass(slot):
            block = res.at[PLACE[slot], half_at(c)]
            res_mate[slot] = send(block, block, partner)

        res_pass(0)
        wide_q = rq.at[quart_at(j)]
        rq_sent = [send(wide_q, wide_q, dev) for dev in (partner, facing, across)]
        for stream in (0, 1):
            for way in (1, -1):
                res_z[way, 2, stream].wait_recv()
                if (way == 1) == (stream == 0):
                    res_send(way, 4, stream, 2)
                res_send(way, 3, stream, 1)
        for dist in (1, 2, 3):
            for way in (1, -1):
                if dist != 2:
                    res_z[way, dist, 0].wait_recv()
                    res_z[way, dist, 1].wait_recv()
                res_pass((-way * dist) % RING)
        res_z[1, 4, 0].wait_recv()
        res_z[-1, 4, 1].wait_recv()
        res_pass(4)

    def res_ready(slots):
        if zs:
            for s in slots:
                res_mate[s].wait_recv()

    def gradient(p0, n, first):
        cols = slice(p0 * lanes, (p0 + n) * lanes)
        left = jnp.concatenate([res[p, 0:og, :] for p in range(p0, p0 + n)], axis=1)

        def part(n0, width):
            n0 = pl.multiple_of(n0, 128)
            term = dot(left, kt[pl.ds(n0, width), cols], NT)
            if first:
                gp[:, pl.ds(n0, width)] = term
            else:
                gpb[:, pl.ds(n0, width)] = (gp[:, pl.ds(n0, width)] + term).astype(BF16)

        over(pm // 256, lambda n0: part(n0, 256))
        part(pm, pp - pm)

    res_ready((0, 1, 7, 2, 6, 3))
    gradient(0, 6, True)
    res_ready((5, 4))
    gradient(6, 2, False)

    def own_term(s):
        col = lax.rem(y + s + RING, RING) * chunk
        return dot(gpb[...], oht[:, pl.ds(pl.multiple_of(col, 128), chunk)], NN)

    rows_p, rows_q = slice(0, top), slice(top, og)
    first_p = {1: slice(0, mid_p), -1: slice(mid_p, top)}
    first_q = {1: slice(top, mid_q), -1: slice(mid_q, og)}
    if ys:
        beside = at_y(y, 1 - xl)
        chain = {}
        swap = {}

        def term(s):
            whole = own_term(s)
            for h in (0, 1):
                terms[s % RING, h] = whole[:, h * sub : (h + 1) * sub]
            xps[s % RING] = terms[s % RING, 1 - xl, rows_p, :].astype(BF16)
            swap[s % RING] = send(xps.at[s % RING], xpr.at[s % RING], beside)

        def pass_on(kind, t, own, part, first, buffer, landed, h):
            for w, way in enumerate((1, -1)):
                s = (way * (5 - t)) % RING
                mine = own(s)
                base = part.start
                near_rows = slice(first[way].start - base, first[way].stop - base)
                out_at, in_at = buffer.at[w, t - 1, h], landed.at[w, t - 1, h]
                if t == 1:
                    out_at, in_at = out_at.at[near_rows], in_at.at[near_rows]
                    buffer[w, 0, h, near_rows, :] = mine[near_rows].astype(BF16)
                else:
                    chain[kind, way, t - 1, h].wait_recv()
                    if t == 2:
                        other = first[-way]
                        far_rows = slice(other.start - base, other.stop - base)
                        buffer[w, 1, h, near_rows, :] = (
                            mine[near_rows] + landed[w, 0, h, near_rows, :].astype(F32)
                        ).astype(BF16)
                        buffer[w, 1, h, far_rows, :] = mine[far_rows].astype(BF16)
                    else:
                        buffer[w, t - 1, h] = (
                            mine + landed[w, t - 2, h].astype(F32)
                        ).astype(BF16)
                chain[kind, way, t, h] = send(out_at, in_at, at_y(y + way, xl))

        def pass_q(t):
            for h in (0, 1):
                pass_on(
                    "q", t, lambda s, h=h: terms[s, h, rows_q, :], rows_q, first_q, yqs, yqr, h
                )

        def both_x(s):
            if s in swap:
                swap.pop(s).wait_recv()
                terms[s, xl, rows_p, :] += xpr[s].astype(F32)
            return terms[s, xl, rows_p, :]

        def pass_p(t):
            pass_on("p", t, both_x, rows_p, first_p, yps, ypr, 0)

        term(4)
        pass_q(1)
        term(3)
        term(5)
        pass_q(2)
        pass_p(1)
        term(2)
        term(6)
        pass_q(3)
        pass_p(2)
        term(1)
        term(7)
        pass_q(4)
        term(0)
        pass_p(3)
        for h in (0, 1):
            chain["q", 1, 4, h].wait_recv()
            chain["q", -1, 4, h].wait_recv()
            terms[0, h, rows_q, :] += yqr[0, 3, h].astype(F32) + yqr[1, 3, h].astype(F32)
        xsend[...] = terms[0, 1 - xl, rows_q, :].astype(BF16)
        swap_q = send(xsend, xrecv, beside)
        pass_p(4)
        sum_p = both_x(0)
        chain["p", 1, 4, 0].wait_recv()
        chain["p", -1, 4, 0].wait_recv()
        sum_p = sum_p + ypr[0, 3, 0].astype(F32) + ypr[1, 3, 0].astype(F32)
        grad[0, xl, rows_p, :] = sum_p.astype(BF16)
        back = {}

        def copy_back(part, way, level):
            h = 1 - xl if part == "b" else xl
            rows_of = rows_p if part == "p" else rows_q
            here = slot_of(way, level - 1) % RING
            back[part, way, level] = send(
                grad.at[here, h, rows_of], grad.at[slot_of(way, level), h, rows_of],
                at_y(y + way, xl),
            )

        def give(slot, rows_of=rows_p):
            block = grad.at[slot, xl, rows_of]
            return send(block, block, beside)

        copy_back("p", 1, 1)
        copy_back("p", -1, 1)
        beside_sent = {0: give(0)}
        swap_q.wait_recv()
        grad[0, xl, rows_q, :] = (terms[0, xl, rows_q, :] + xrecv[...].astype(F32)).astype(BF16)
        beside_q = give(0, rows_q)
        copy_back("q", 1, 1)
        copy_back("q", -1, 1)
    else:
        for s in range(RING):
            for h in (0, 1):
                grad[s, h] = own_term(s)[:, h * sub : (h + 1) * sub].astype(BF16)

    stores = []

    def store(s, h):
        col = lax.rem(y + s, RING) * chunk + h * sub
        copy = pltpu.make_async_copy(
            grad.at[s, h],
            grad_out.at[:, pl.ds(pl.multiple_of(col, 128), sub)],
            osem.at[len(stores)],
        )
        copy.start()
        stores.append(copy)

    if ys:
        store(0, xl)
        beside_q.wait_recv()
        copy_back("b", 1, 1)
        copy_back("b", -1, 1)
        beside_sent[0].wait_recv()
        store(0, 1 - xl)
        for level in range(1, 5):
            for part in ("p", "q", "b"):
                only = 1 if part == "p" else -1
                for way in (1, -1) if level < 4 else (only,):
                    slot = slot_of(way, level)
                    back[part, way, level].wait_recv()
                    if level < 3 or (level == 3 and way == only):
                        copy_back(part, way, level + 1)
                    if part == "p":
                        beside_sent[slot] = give(slot)
                    elif part == "q":
                        store(slot, xl)
            if level == 1 and zs:
                for copy in rq_sent:
                    copy.wait_recv()
                rt[...] = rq[...].T
                res_out[...] = rt[rows_at(j), 0:out]
        for slot in (7, 1, 6, 2, 5, 3, 4):
            beside_sent[slot].wait_recv()
            store(slot, 1 - xl)
    else:
        for s in range(RING):
            for h in (0, 1):
                store(s, h)
        if zs:
            for copy in rq_sent:
                copy.wait_recv()
        rt[...] = rq[...].T
        res_out[...] = rt[rows_at(j), 0:out]
    for copy in stores:
        copy.wait()
    for copy in started:
        copy.wait_send()


def on_device(zs, ys, bpool, bidx, cpool, cidx, tgt, coef):
    rows, d = bidx.shape[0], bpool.shape[1]
    out, cen = tgt.shape[1], cidx.shape[0]
    n_pool = cpool.shape[0]
    outp, og = up(out, 64), up(out, 16)
    pp = n_pool // 256 * 256 + 128
    lanes = 4 * rows
    half, quart = outp // 2, outp // 4
    wide = up(outp, 128)
    chunk = cen // RING
    sub = chunk // 2
    top = up(og * 9 // 16, 16)
    vmem = pl.BlockSpec(memory_space=pltpu.VMEM)
    hbm = pl.BlockSpec(memory_space=pl.ANY)
    tail = pl.BlockSpec((16, d), lambda i: (n_pool // 256 * 16, 0))
    grad, residual = pl.pallas_call(
        functools.partial(step_kernel, zs, ys),
        out_shape=(
            jax.ShapeDtypeStruct((og, cen), BF16),
            jax.ShapeDtypeStruct((rows, out), F32),
        ),
        grid=(1,),
        in_specs=[vmem, vmem, vmem, hbm, tail, vmem, hbm],
        out_specs=(hbm, vmem),
        scratch_shapes=[
            pltpu.VMEM((up(bpool.shape[0], 16), d), BF16),
            pltpu.VMEM((RING, lanes, d), BF16),
            pltpu.VMEM((up(n_pool, 16), d), BF16),
            pltpu.VMEM((pp, 128), F32),
            pltpu.VMEM((pp, cen), BF16),
            pltpu.VMEM((out, cen), F32),
            pltpu.VMEM((og, cen), BF16),
            pltpu.VMEM((outp, pp), BF16),
            pltpu.VMEM((pp, RING * lanes), BF16),
            pltpu.VMEM((outp, RING * lanes), F32),
            pltpu.VMEM((RING, half, lanes), BF16),
            pltpu.VMEM((RING, half, lanes), BF16),
            pltpu.VMEM((RING, 2, quart, lanes), BF16),
            pltpu.VMEM((RING, 2, quart, lanes), BF16),
            pltpu.VMEM((lanes, wide), F32),
            pltpu.VMEM((wide, lanes), F32),
            pltpu.VMEM((RING, outp, lanes), BF16),
            pltpu.VMEM((outp, lanes), F32),
            pltpu.VMEM((lanes, outp), F32),
            pltpu.VMEM((og, pp), F32),
            pltpu.VMEM((og, pp), BF16),
            pltpu.VMEM((RING, 2, og, sub), F32),
            pltpu.VMEM((RING, top, sub), BF16),
            pltpu.VMEM((RING, top, sub), BF16),
            pltpu.VMEM((2, 4, 1, top, sub), BF16),
            pltpu.VMEM((2, 4, 1, top, sub), BF16),
            pltpu.VMEM((2, 4, 2, og - top, sub), BF16),
            pltpu.VMEM((2, 4, 2, og - top, sub), BF16),
            pltpu.VMEM((og - top, sub), BF16),
            pltpu.VMEM((og - top, sub), BF16),
            pltpu.VMEM((RING, 2, og, sub), BF16),
            pltpu.SemaphoreType.DMA((COPIES,)),
            pltpu.SemaphoreType.DMA((COPIES,)),
            pltpu.SemaphoreType.DMA((2,)),
            pltpu.SemaphoreType.DMA((2 * RING,)),
        ],
        compiler_params=pltpu.CompilerParams(
            collective_id=0, has_side_effects=True, vmem_limit_bytes=62 * 1024 * 1024
        ),
        name="regression_step",
    )(
        bidx.reshape(1, rows), bpool, cidx.reshape(1, cen), cpool, cpool, tgt, coef.T,
    )
    batch_total = rows * lax.axis_size("batch") * lax.axis_size("centre")
    step_size = 8.0 / math.sqrt(batch_total)
    updated = coef - step_size * grad[:out].astype(F32).T
    return updated, residual


def solution(mesh):
    both = ("batch", "centre")
    zs, ys = mesh.shape["centre"] > 1, mesh.shape["batch"] > 1
    return jax.shard_map(
        functools.partial(on_device, zs, ys),
        mesh=mesh,
        in_specs=(
            P(both, None), P(both), P("centre", None), P("centre"), P(both, None), P("centre", None),
        ),
        out_specs=(P("centre", None), P(both, None)),
        check_vma=False,
    )
```
